128 devices in a mesh: task: 4 (over y), param: 32 (over z, x, core).
Axes of the slice: x: 4, y: 4, z: 4, core: 2. Of those that a mesh axis runs over, the one named last changes fastest.
Arguments:
- grads: bfloat16 [8, 8192, 4096], P('task', 'param')
- order: int32 [8], replicated, may hold values from 0 to 7, each once
Outputs:
- update: float32 [8192, 4096], P('param', 'task')
The draws below stay inside these ranges and needn't reach their ends.
All inputs are finite; a program needn't handle non-finite values.
Results may differ from the reference program's by a relative error of at most 0.0003.
Values may be sent and summed in bfloat16 or wider, within the bound.
No kernel may reach another device: no remote copies, remote signals or barrier semaphores. Data moves between devices by JAX's collectives and lax.ppermute only.
A program may use at most 64 MiB of HBM per device.

```python
import jax
import jax.numpy as jnp
from jax import lax

FF = 4096
ROW_DEV = 256
TASKS = 8
ROWS = 8192


def draw_grads(key, part):
    keys = jax.random.split(jax.random.fold_in(key, 11), 5)
    blocks = ROWS // ROW_DEV
    cols = FF // 8
    base = jax.random.uniform(keys[0], (TASKS, blocks, 1, 8, 1), jnp.float32, -1.5, 1.5)
    row_part = jax.random.uniform(keys[4], (TASKS, blocks, ROW_DEV, 8, 1), jnp.float32, -2.0, 2.0)
    mixing = base + row_part
    shared = jax.random.normal(keys[1], (1, blocks, ROW_DEV, 8, cols), jnp.float32)
    noise = jax.random.normal(keys[2], (TASKS, blocks, ROW_DEV, 8, cols), jnp.float32)
    scales = jnp.exp(jax.random.uniform(keys[3], (1, blocks, 1, 8, 1), jnp.float32, 0.0, 2.3))
    values = (mixing * shared + noise) * scales
    return values.reshape(TASKS, ROWS, FF).astype(jnp.bfloat16)


def setup_inputs(seed: int = 0) -> dict:
    key_of = jax.random.split(jax.random.key(seed), 3)
    return {
        "grads": draw_grads(jax.random.fold_in(key_of[2], 71), 0),
        "order": jax.random.permutation(key_of[1], TASKS).astype(jnp.int32),
    }


def reference(grads, order):
    flat = grads.reshape(TASKS, -1)
    gram = lax.dot_general(flat, flat, (((1,), (1,)), ((), ())), preferred_element_type=jnp.float32)
    coefs = jnp.eye(TASKS, dtype=jnp.float32)
    labels = jnp.arange(TASKS, dtype=jnp.int32)
    for k in range(TASKS):
        j = order[k]
        picked = (labels == j).astype(jnp.float32)
        column = lax.optimization_barrier(jnp.sum(gram * picked[None, :], axis=1))
        d = lax.optimization_barrier(jnp.sum(coefs * column[None, :], axis=1))
        norm_j = jnp.sum(column * picked)
        w = jnp.minimum(d, 0.0) / (norm_j + 1e-06)
        w = w * (1.0 - picked)
        coefs = coefs - w[:, None] * picked[None, :]
    weight = lax.optimization_barrier(jnp.sum(coefs, axis=0))
    combined = jnp.zeros((ROWS, FF), jnp.float32)
    for m in range(TASKS):
        combined = combined + weight[m] * grads[m].astype(jnp.float32)
    rms = jnp.sqrt(jnp.sum(combined * combined) / (ROWS * FF) + 1e-06)
    return combined * (0.5 / rms)
```

```python
import functools

import jax
import jax.numpy as jnp
from jax import lax
from jax.experimental import pallas as pl
from jax.experimental.pallas import tpu as pltpu
from jax.sharding import Mesh
from jax.sharding import PartitionSpec as P

PARAM = ("param_0", "param_1", "param_2")
TASK_PARAM = ("task", *PARAM)
CHUNKS = (64, 128, 64)
GRAIN = 16
OUT_ROWS = 64
LANES = 128
SUBLANES = 8
EPS = 1e-06
VMEM = pl.BlockSpec(memory_space=pltpu.VMEM)
SMEM = pl.BlockSpec(memory_space=pltpu.SMEM)


def places(order_ref, place_ref, tasks):
    for k in range(tasks):
        place_ref[order_ref[k]] = k


def slot_places(place_ref, me, parts, per):
    found = []
    for s in range(parts):
        first = lax.rem(me + (parts - s), parts) * per
        found += [place_ref[first + u] for u in range(per)]
    return found


def gram_kernel(parts, per, row0, first, last, order_ref, me_ref, own_ref, *refs):
    got, refs = refs[: parts - 1], refs[parts - 1 :]
    if not first:
        before_ref, refs = refs[0], refs[1:]
    out_ref, place_ref, *scratch = refs
    acc_ref = scratch[0] if last else out_ref
    tasks = parts * per
    rows, width = got[0].shape[1:]
    places(order_ref, place_ref, tasks)
    at = slot_places(place_ref, me_ref[0], parts, per)
    pairs = [(i, j) for i in range(tasks) for j in range(i, tasks)]

    def body(r, sums):
        sums = list(sums)
        for c in range(width // LANES):
            cols = pl.ds(c * LANES, LANES)
            x = [own_ref[u, pl.ds(row0 + r * GRAIN, GRAIN), cols] for u in range(per)]
            x += [g[u, pl.ds(r * GRAIN, GRAIN), cols] for g in got for u in range(per)]
            x = [v.astype(jnp.float32) for v in x]
            for h in range(GRAIN // SUBLANES):
                part = [v[h * SUBLANES : (h + 1) * SUBLANES] for v in x]
                for p, (i, j) in enumerate(pairs):
                    sums[p] = sums[p] + part[i] * part[j]
        return tuple(sums)

    zero = jnp.zeros((SUBLANES, LANES), jnp.float32)
    sums = lax.fori_loop(0, rows // GRAIN, body, (zero,) * len(pairs))
    square = tasks * tasks
    for p, (i, j) in enumerate(pairs):
        for a, b in ((i, j), (j, i))[: 1 if i == j else 2]:
            acc_ref[pl.ds(at[a] * tasks + at[b], SUBLANES, stride=square), :] = sums[p]
    if not first:
        acc_ref[...] += before_ref[...]
    if last:
        folded = acc_ref[:square, :]
        for k in range(1, SUBLANES):
            folded = folded + acc_ref[k * square : (k + 1) * square, :]
        folded = jnp.concatenate([folded, jnp.zeros((LANES - square, LANES), jnp.float32)], axis=0)
        row = lax.dot_general(
            jnp.ones((SUBLANES, LANES), jnp.float32), folded, (((1,), (1,)), ((), ())),
            precision=lax.Precision.HIGHEST, preferred_element_type=jnp.float32,
        )
        out_ref[...] = jnp.broadcast_to(row[:1], out_ref.shape)


def gram_of(order, me, own, got, before, row0, devices, last):
    per = own.shape[0]
    parts = len(got) + 1
    table = (SUBLANES * (parts * per) ** 2, LANES)
    first = before is None
    return pl.pallas_call(
        functools.partial(gram_kernel, parts, per, row0, first, last),
        in_specs=[SMEM, SMEM] + [VMEM] * (parts + (0 if first else 1)),
        out_specs=VMEM,
        out_shape=jax.ShapeDtypeStruct((devices, LANES) if last else table, jnp.float32),
        scratch_shapes=[pltpu.SMEM((parts * per,), jnp.int32)]
        + ([pltpu.VMEM(table, jnp.float32)] if last else []),
        compiler_params=pltpu.CompilerParams(vmem_limit_bytes=4 << 20),
        name="gram",
    )(order, me, own, *got, *([] if first else [before]))


def combine_kernel(parts, per, entries, order_ref, me_ref, gram_ref, own_ref, *refs):
    refs, (out_ref, place_ref, w_ref) = refs[:-3], refs[-3:]
    tasks = parts * per
    got = [refs[k : k + parts - 1] for k in range(0, len(refs), parts - 1)]
    step = pl.program_id(0)

    @pl.when(step == 0)
    def _():
        places(order_ref, place_ref, tasks)
        flat = jnp.sum(gram_ref[...], axis=0, keepdims=True)
        lane = lax.broadcasted_iota(jnp.int32, (tasks, LANES), 1)
        sub = lax.broadcasted_iota(jnp.int32, (tasks, LANES), 0)
        gram = jnp.concatenate(
            [pltpu.roll(flat, (LANES - tasks * k) % LANES, 1) for k in range(tasks)], axis=0
        )
        gram = jnp.where(lane < tasks, gram, 0.0)
        eye = lane == sub
        norm = jnp.sum(jnp.where(eye, gram, 0.0), axis=1, keepdims=True)
        inverse = jnp.broadcast_to(1.0 / (norm + EPS), (tasks, LANES))
        columns = [jnp.broadcast_to(gram[:, k : k + 1], (tasks, LANES)) for k in range(tasks)]
        coefs, dots = eye.astype(jnp.float32), gram
        for k in range(tasks):
            w = jnp.minimum(dots[k : k + 1, :], 0.0) * inverse[k : k + 1, :]
            w = jnp.broadcast_to(jnp.where(lane[:1] == k, 0.0, w), (tasks, LANES))
            coefs = coefs - jnp.where(sub == k, w, 0.0)
            dots = dots - columns[k] * w
        weight = jnp.sum(coefs, axis=1, keepdims=True)
        energy = jnp.sum(weight * jnp.sum(dots, axis=1, keepdims=True), axis=0, keepdims=True)
        rms = jnp.sqrt(jnp.maximum(energy, 0.0) / entries + EPS)
        w_ref[...] = jnp.broadcast_to(weight * (0.5 / rms), (tasks, LANES))

    at = slot_places(place_ref, me_ref[0], parts, per)
    weights = [jnp.broadcast_to(w_ref[pl.ds(a, 1), :], (GRAIN, LANES)) for a in at]
    width = out_ref.shape[1]
    row0 = 0
    for blocks in got:
        for top in range(0, blocks[0].shape[1], OUT_ROWS):

            @pl.when(step == (row0 + top) // OUT_ROWS)
            def _():
                for r in range(0, OUT_ROWS, GRAIN):
                    for c in range(0, width, LANES):
                        total = None
                        for s in range(parts):
                            for u in range(per):
                                if s == 0:
                                    x = own_ref[u, row0 + top + r : row0 + top + r + GRAIN, c : c + LANES]
                                else:
                                    x = blocks[s - 1][u, top + r : top + r + GRAIN, c : c + LANES]
                                term = weights[s * per + u] * x.astype(jnp.float32)
                                total = term if total is None else total + term
                        out_ref[r : r + GRAIN, c : c + LANES] = total

        row0 += blocks[0].shape[1]


def combine(order, me, gram, own, received, entries):
    per, rows, block = own.shape
    parts = len(received[0]) + 1
    flat = [b for got in received for b in got]
    return pl.pallas_call(
        functools.partial(combine_kernel, parts, per, entries),
        grid=(rows // OUT_ROWS,),
        in_specs=[SMEM, SMEM] + [VMEM] * (2 + len(flat)),
        out_specs=pl.BlockSpec((OUT_ROWS, block), lambda i: (i, 0)),
        out_shape=jax.ShapeDtypeStruct((rows, block), jnp.float32),
        scratch_shapes=[
            pltpu.SMEM((parts * per,), jnp.int32),
            pltpu.VMEM((parts * per, LANES), jnp.float32),
        ],
        compiler_params=pltpu.CompilerParams(vmem_limit_bytes=4 << 20),
        name="combine",
    )(order, me, gram, own, *flat)


def near(value):
    return pltpu.with_memory_space_constraint(value, pltpu.VMEM)


def shift(value, axis, by):
    n = lax.axis_size(axis)
    return near(lax.ppermute(value, axis, [(i, (i + by) % n) for i in range(n)]))


def shards(grads, order):
    per, rows, width = grads.shape
    parts, devices = lax.axis_size("task"), lax.axis_size(TASK_PARAM)
    block = width // parts
    entries = rows * lax.axis_size(PARAM) * width
    index = lax.axis_index("task")
    me = index.astype(jnp.int32).reshape(1)
    received, row0 = [], 0
    for size in CHUNKS:
        got = {}
        for s in (2, 1, 3):
            to = lax.rem(index + s, parts) * block
            got[s] = shift(lax.dynamic_slice(grads, (0, row0, to), (per, size, block)), "task", s)
        received.append([got[s] for s in (1, 2, 3)])
        row0 += size
    own = near(lax.dynamic_slice(grads, (0, 0, index * block), (per, rows, block)))
    gram, row0 = None, 0
    for size, got in zip(CHUNKS, received):
        gram = gram_of(order, me, own, got, gram, row0, devices, row0 + size == rows)
        row0 += size
    gram = lax.all_to_all(gram, TASK_PARAM, 0, 0, tiled=True)
    return combine(order, me, gram, own, received, entries)


def solution(mesh):
    torus = Mesh(
        mesh.devices.reshape(mesh.shape["task"], 4, 4, 2), ("task", "param_0", "param_1", "param_2")
    )
    in_specs = (P("task", PARAM, None), P())
    out_specs = P(PARAM, "task")
    return jax.shard_map(
        shards, mesh=torus, in_specs=in_specs, out_specs=out_specs, check_vma=False
    )
```

```python
import functools

import jax
import jax.numpy as jnp
from jax import lax
from jax.experimental import pallas as pl
from jax.experimental.pallas import tpu as pltpu
from jax.sharding import Mesh
from jax.sharding import PartitionSpec as P

PARAM = ("param_0", "param_1", "param_2")
TASK_PARAM = ("task", *PARAM)
CHUNKS = (192, 64)
GRAIN = 16
OUT_ROWS = 64
LANES = 128
SUBLANES = 8
EPS = 1e-06
VMEM = pl.BlockSpec(memory_space=pltpu.VMEM)
SMEM = pl.BlockSpec(memory_space=pltpu.SMEM)


def slot_tasks(parts, per):
    me = lax.axis_index("task")
    return [lax.rem(me + (parts - s), parts) * per + u for s in range(parts) for u in range(per)]


def tables(order_ref, slots, select_ref, pick_ref):
    tasks = len(slots)
    left = lax.broadcasted_iota(jnp.int32, (LANES, LANES), 0)
    right = lax.broadcasted_iota(jnp.int32, (LANES, LANES), 1)
    first, second = jnp.full((LANES, LANES), -1, jnp.int32), jnp.zeros((LANES, LANES), jnp.int32)
    place = lax.broadcasted_iota(jnp.int32, (tasks, LANES), 0)
    ordered = jnp.zeros((tasks, LANES), jnp.int32)
    for k in range(tasks):
        first = jnp.where(right // tasks == k, order_ref[k], first)
        second = jnp.where(right % tasks == k, order_ref[k], second)
        ordered = jnp.where(place == k, order_ref[k], ordered)
    meet = (first >= 0) & (left == first * tasks + second)
    select_ref[...] = jnp.where(meet, 1.0, 0.0)
    for i, task in enumerate(slots):
        pick_ref[i] = jnp.where(ordered == task, 1.0, 0.0)


def gram_kernel(parts, per, row0, first, last, *refs):
    if first:
        order_ref, refs = refs[0], refs[1:]
    own_ref, got, refs = refs[0], refs[1:parts], refs[parts:]
    if not first:
        before_ref, refs = refs[0], refs[1:]
    out_ref, *refs = refs
    acc_ref = refs[-1] if last else out_ref
    tasks = parts * per
    rows, width = got[0].shape[1:]
    slots = slot_tasks(parts, per)
    pairs = [(i, j) for i in range(tasks) for j in range(i, tasks)]

    def body(r, sums):
        sums = list(sums)
        for c in range(width // LANES):
            cols = pl.ds(c * LANES, LANES)
            x = [own_ref[u, pl.ds(row0 + r * GRAIN, GRAIN), cols] for u in range(per)]
            x += [g[u, pl.ds(r * GRAIN, GRAIN), cols] for g in got for u in range(per)]
            x = [v.astype(jnp.float32) for v in x]
            for h in range(GRAIN // SUBLANES):
                part = [v[h * SUBLANES : (h + 1) * SUBLANES] for v in x]
                for p, (i, j) in enumerate(pairs):
                    sums[p] = sums[p] + part[i] * part[j]
        return tuple(sums)

    zero = jnp.zeros((SUBLANES, LANES), jnp.float32)
    sums = lax.fori_loop(0, rows // GRAIN, body, (zero,) * len(pairs))
    square = tasks * tasks
    for p, (i, j) in enumerate(pairs):
        for a, b in ((i, j), (j, i))[: 1 if i == j else 2]:
            acc_ref[pl.ds(slots[a] * tasks + slots[b], SUBLANES, stride=square), :] = sums[p]
    if not first:
        acc_ref[...] += before_ref[...]
    if first:
        tables(order_ref, slots, *refs[:2])
    if last:
        folded = acc_ref[:square, :]
        for k in range(1, SUBLANES):
            folded = folded + acc_ref[k * square : (k + 1) * square, :]
        folded = jnp.concatenate([folded, jnp.zeros((LANES - square, LANES), jnp.float32)], axis=0)
        row = lax.dot_general(
            jnp.ones((SUBLANES, LANES), jnp.float32), folded, (((1,), (1,)), ((), ())),
            precision=lax.Precision.HIGHEST, preferred_element_type=jnp.float32,
        )
        out_ref[...] = jnp.broadcast_to(row[:1], out_ref.shape)


def gram_of(order, own, got, before, row0, devices, last):
    per = own.shape[0]
    parts = len(got) + 1
    tasks = parts * per
    table = (SUBLANES * tasks**2, LANES)
    first = before is None
    shapes = [(devices, LANES) if last else table]
    if first:
        shapes += [(LANES, LANES), (tasks, tasks, LANES)]
    return pl.pallas_call(
        functools.partial(gram_kernel, parts, per, row0, first, last),
        in_specs=[SMEM] * first + [VMEM] * (parts + (not first)),
        out_specs=[VMEM] * len(shapes),
        out_shape=[jax.ShapeDtypeStruct(shape, jnp.float32) for shape in shapes],
        scratch_shapes=[pltpu.VMEM(table, jnp.float32)] if last else [],
        compiler_params=pltpu.CompilerParams(vmem_limit_bytes=4 << 20),
        name="gram",
    )(*([order] if first else []), own, *got, *([] if first else [before]))


def combine_kernel(parts, per, entries, gram_ref, select_ref, pick_ref, own_ref, *refs):
    refs, (out_ref, rows_ref, sems) = refs[:-3], refs[-3:]
    tasks = parts * per
    got = [refs[k : k + parts - 1] for k in range(0, len(refs), parts - 1)]
    flat = jnp.sum(gram_ref[...], axis=0, keepdims=True)
    flat = lax.dot_general(
        jnp.broadcast_to(flat, (SUBLANES, LANES)), select_ref[...], (((1,), (0,)), ((), ())),
        precision=lax.Precision.HIGHEST, preferred_element_type=jnp.float32,
    )[:1]
    lane = lax.broadcasted_iota(jnp.int32, (tasks, LANES), 1)
    sub = lax.broadcasted_iota(jnp.int32, (tasks, LANES), 0)
    gram = jnp.concatenate(
        [pltpu.roll(flat, (LANES - tasks * k) % LANES, 1) for k in range(tasks)], axis=0
    )
    gram = jnp.where(lane < tasks, gram, 0.0)
    eye = lane == sub
    norm = jnp.sum(jnp.where(eye, gram, 0.0), axis=1, keepdims=True)
    inverse = jnp.broadcast_to(1.0 / (norm + EPS), (tasks, LANES))
    columns = [jnp.broadcast_to(gram[:, k : k + 1], (tasks, LANES)) for k in range(tasks)]
    coefs, dots = eye.astype(jnp.float32), gram
    for k in range(tasks):
        w = jnp.minimum(dots[k : k + 1, :], 0.0) * inverse[k : k + 1, :]
        w = jnp.broadcast_to(jnp.where(lane[:1] == k, 0.0, w), (tasks, LANES))
        coefs = coefs - jnp.where(sub == k, w, 0.0)
        dots = dots - columns[k] * w
    weight = jnp.sum(coefs, axis=1, keepdims=True)
    energy = jnp.sum(weight * jnp.sum(dots, axis=1, keepdims=True), axis=0, keepdims=True)
    rms = jnp.sqrt(jnp.maximum(energy, 0.0) / entries + EPS)
    weight = jnp.broadcast_to(weight * (0.5 / rms), (tasks, LANES))
    weights = [
        jnp.broadcast_to(jnp.sum(pick_ref[i] * weight, axis=0, keepdims=True), (GRAIN, LANES))
        for i in range(tasks)
    ]
    width = rows_ref.shape[1]
    copies, row0 = [], 0
    for blocks in got:
        size = blocks[0].shape[1]
        for top in range(0, size, OUT_ROWS):
            here = min(OUT_ROWS, size - top)

            def body(r, _):
                at = pl.multiple_of(top + r * GRAIN, GRAIN)
                for c in range(0, width, LANES):
                    cols = pl.ds(c, LANES)
                    total = None
                    for s in range(parts):
                        for u in range(per):
                            if s == 0:
                                x = own_ref[u, pl.ds(row0 + at, GRAIN), cols]
                            else:
                                x = blocks[s - 1][u, pl.ds(at, GRAIN), cols]
                            term = weights[s * per + u] * x.astype(jnp.float32)
                            total = term if total is None else total + term
                    rows_ref[pl.ds(row0 + at, GRAIN), cols] = total
                return 0

            lax.fori_loop(0, here // GRAIN, body, 0)
            span = pl.ds(row0 + top, here)
            copy = pltpu.make_async_copy(rows_ref.at[span], out_ref.at[span], sems.at[len(copies)])
            copy.start()
            copies.append(copy)
        row0 += size
    for copy in copies:
        copy.wait()


def combine(gram, select, pick, own, received, entries):
    per, rows, block = own.shape
    parts = len(received[0]) + 1
    flat = [b for got in received for b in got]
    pieces = sum(-(-got[0].shape[1] // OUT_ROWS) for got in received)
    return pl.pallas_call(
        functools.partial(combine_kernel, parts, per, entries),
        in_specs=[VMEM] * (4 + len(flat)),
        out_specs=pl.BlockSpec(memory_space=pltpu.HBM),
        out_shape=jax.ShapeDtypeStruct((rows, block), jnp.float32),
        scratch_shapes=[
            pltpu.VMEM((rows, block), jnp.float32),
            pltpu.SemaphoreType.DMA((pieces,)),
        ],
        compiler_params=pltpu.CompilerParams(vmem_limit_bytes=4 << 20),
        name="combine",
    )(gram, select, pick, own, *flat)


def cut_kernel(parts, shifts, spans, grads_ref, *refs):
    outs, sems = refs[:-1], refs[-1]
    block = outs[0].shape[-1]
    me = lax.axis_index("task")
    copies = []
    for row0, size in spans:
        for s in shifts:
            column = pl.multiple_of(lax.rem(me + s, parts) * block, block)
            source = grads_ref.at[:, pl.ds(row0, size), pl.ds(column, block)]
            k = len(copies)
            copies.append(pltpu.make_async_copy(source, outs[k], sems.at[k]))
    for copy in copies:
        copy.start()
    for copy in copies:
        copy.wait()


def cut(grads, parts, shifts, spans):
    per, _, width = grads.shape
    shapes = [(per, size, width // parts) for _, size in spans for _ in shifts]
    cuts = pl.pallas_call(
        functools.partial(cut_kernel, parts, shifts, spans),
        in_specs=[pl.BlockSpec(memory_space=pltpu.HBM)],
        out_specs=[VMEM] * len(shapes),
        out_shape=[pltpu.VMEM(shape, grads.dtype) for shape in shapes],
        scratch_shapes=[pltpu.SemaphoreType.DMA((len(shapes),))],
        compiler_params=pltpu.CompilerParams(vmem_limit_bytes=4 << 20),
        name="cut",
    )(pltpu.with_memory_space_constraint(grads, pltpu.HBM))
    return [near(c) for c in cuts]


def near(value):
    return pltpu.with_memory_space_constraint(value, pltpu.VMEM)


def shift(value, axis, by):
    n = lax.axis_size(axis)
    return near(lax.ppermute(value, axis, [(i, (i + by) % n) for i in range(n)]))


def shards(grads, order):
    per, rows, width = grads.shape
    parts, devices = lax.axis_size("task"), lax.axis_size(TASK_PARAM)
    entries = rows * lax.axis_size(PARAM) * width
    shifts, received, row0 = (2, 1, 3), [], 0
    for size in CHUNKS:
        cuts = cut(grads, parts, shifts, [(row0, size)])
        got = {s: shift(c, "task", s) for s, c in zip(shifts, cuts)}
        received.append([got[s] for s in range(1, parts)])
        row0 += size
    own = cut(grads, parts, (0,), [(0, rows)])[0]
    gram, row0 = None, 0
    for size, got in zip(CHUNKS, received):
        gram, *more = gram_of(order, own, got, gram, row0, devices, row0 + size == rows)
        if more:
            select, pick = more
        row0 += size
    gram = lax.all_to_all(gram, TASK_PARAM, 0, 0, tiled=True)
    return combine(gram, select, pick, own, received, entries)


def solution(mesh):
    torus = Mesh(
        mesh.devices.reshape(mesh.shape["task"], 4, 4, 2), ("task", "param_0", "param_1", "param_2")
    )
    in_specs = (P("task", PARAM, None), P())
    out_specs = P(PARAM, "task")
    return jax.shard_map(
        shards, mesh=torus, in_specs=in_specs, out_specs=out_specs, check_vma=False
    )
```

```python
import functools

import jax
import jax.numpy as jnp
from jax import lax
from jax.experimental import pallas as pl
from jax.experimental.pallas import tpu as pltpu
from jax.sharding import Mesh
from jax.sharding import PartitionSpec as P

PARAM = ("param_0", "param_1", "param_2")
TASK_PARAM = ("task", *PARAM)
CHUNKS = (192, 64)
SHIFTS = (2, 1, 3)
GROUPS = (((2, 0, 256), (1, 0, 192), (3, 0, 192)), ((1, 192, 64), (3, 192, 64)))
GRAIN = 16
OUT_ROWS = 64
LANES = 128
SUBLANES = 8
EPS = 1e-06
VMEM = pl.BlockSpec(memory_space=pltpu.VMEM)
SMEM = pl.BlockSpec(memory_space=pltpu.SMEM)


def slot_tasks(parts, per):
    me = lax.axis_index("task")
    return [lax.rem(me + (parts - s), parts) * per + u for s in (0, *SHIFTS) for u in range(per)]


def tables(order_ref, slots, rows_ref, columns_ref, pick_ref):
    tasks = len(slots)

    def ordered(shape, dim):
        place, task = lax.broadcasted_iota(jnp.int32, shape, dim), jnp.full(shape, -1, jnp.int32)
        for k in range(tasks):
            task = jnp.where(place == k, order_ref[k], task)
        return task

    lane = lax.broadcasted_iota(jnp.int32, rows_ref.shape, 1)
    rows_ref[...] = jnp.where(lane // tasks == ordered(rows_ref.shape, 0), 1.0, 0.0)
    sub = lax.broadcasted_iota(jnp.int32, columns_ref.shape, 0)
    columns_ref[...] = jnp.where(sub % tasks == ordered(columns_ref.shape, 1), 1.0, 0.0)
    for i, task in enumerate(slots):
        pick_ref[i] = jnp.where(ordered(pick_ref.shape[1:], 0) == task, 1.0, 0.0)


def pieces_of(value):
    high = value.astype(jnp.bfloat16)
    rest = value - high.astype(jnp.float32)
    middle = rest.astype(jnp.bfloat16)
    return high, middle, (rest - middle.astype(jnp.float32)).astype(jnp.bfloat16)


def exact_dot(x, y, contract):
    return lax.dot_general(x, y, (contract, ((), ())), preferred_element_type=jnp.float32)


def gram_kernel(parts, per, rows, bases, first, last, *refs):
    if first:
        order_ref, refs = refs[0], refs[1:]
    blocks, refs = refs[:parts], refs[parts:]
    if not first:
        before_ref, refs = refs[0], refs[1:]
    out_ref, *refs = refs
    acc_ref = refs[-1] if last else out_ref
    tasks = parts * per
    width = blocks[0].shape[2]
    slots = slot_tasks(parts, per)
    pairs = [(i, j) for i in range(tasks) for j in range(i, tasks)]

    def body(r, sums):
        sums = list(sums)
        for c in range(width // LANES):
            cols = pl.ds(c * LANES, LANES)
            x = [
                b[u, pl.ds(base + r * GRAIN, GRAIN), cols].astype(jnp.float32)
                for b, base in zip(blocks, bases)
                for u in range(per)
            ]
            for h in range(GRAIN // SUBLANES):
                part = [v[h * SUBLANES : (h + 1) * SUBLANES] for v in x]
                for p, (i, j) in enumerate(pairs):
                    sums[p] = sums[p] + part[i] * part[j]
        return tuple(sums)

    zero = jnp.zeros((SUBLANES, LANES), jnp.float32)
    sums = lax.fori_loop(0, rows // GRAIN, body, (zero,) * len(pairs))
    square = tasks * tasks
    for p, (i, j) in enumerate(pairs):
        for a, b in ((i, j), (j, i))[: 1 if i == j else 2]:
            acc_ref[pl.ds(slots[a] * tasks + slots[b], SUBLANES, stride=square), :] = sums[p]
    if not first:
        acc_ref[...] += before_ref[...]
    if first:
        tables(order_ref, slots, *refs[:3])
    if last:
        folded = acc_ref[:square, :]
        for k in range(1, SUBLANES):
            folded = folded + acc_ref[k * square : (k + 1) * square, :]
        high, middle, low = pieces_of(folded)
        ones = jnp.ones((GRAIN, LANES), jnp.bfloat16)
        row = exact_dot(ones, jnp.concatenate([high, middle], axis=0), ((1,), (1,)))
        row += exact_dot(ones, jnp.concatenate([jnp.zeros_like(low), low], axis=0), ((1,), (1,)))
        out_ref[...] = jnp.broadcast_to(row[:1], out_ref.shape)


def gram_of(order, chunk, rows, before, devices, last):
    blocks, bases = zip(*chunk)
    parts, per = len(blocks), blocks[0].shape[0]
    tasks = parts * per
    table = (SUBLANES * tasks**2, LANES)
    first = before is None
    shapes = [(devices, LANES) if last else table]
    if first:
        shapes += [(tasks, LANES), (LANES, LANES), (tasks, tasks, LANES)]
    return pl.pallas_call(
        functools.partial(gram_kernel, parts, per, rows, bases, first, last),
        in_specs=[SMEM] * first + [VMEM] * (parts + (not first)),
        out_specs=[VMEM] * len(shapes),
        out_shape=[jax.ShapeDtypeStruct(shape, jnp.float32) for shape in shapes],
        scratch_shapes=[pltpu.VMEM(table, jnp.float32)] if last else [],
        compiler_params=pltpu.CompilerParams(vmem_limit_bytes=4 << 20),
        name="gram",
    )(*([order] if first else []), *blocks, *([] if first else [before]))


def combine_kernel(per, entries, chunks, gram_ref, rows_ref, columns_ref, pick_ref, *refs):
    refs, (out_ref, total_ref, sems) = refs[:-3], refs[-3:]
    tasks = rows_ref.shape[0]
    flat = jnp.sum(gram_ref[...], axis=0, keepdims=True)
    flat = flat + pltpu.roll(flat, tasks * tasks, 1)
    pieces = [p.astype(jnp.float32) for p in pieces_of(flat)]
    spread = jnp.concatenate([rows_ref[...] * p for p in pieces], axis=0).astype(jnp.bfloat16)
    found = exact_dot(spread, columns_ref[...].astype(jnp.bfloat16), ((1,), (0,)))
    gram = found[2 * tasks :] + found[tasks : 2 * tasks] + found[:tasks]
    lane = lax.broadcasted_iota(jnp.int32, (tasks, LANES), 1)
    sub = lax.broadcasted_iota(jnp.int32, (tasks, LANES), 0)
    eye = lane == sub
    norm = jnp.sum(jnp.where(eye, gram, 0.0), axis=1, keepdims=True)
    inverse = jnp.broadcast_to(1.0 / (norm + EPS), (tasks, LANES))
    columns = [jnp.broadcast_to(gram[:, k : k + 1], (tasks, LANES)) for k in range(tasks)]
    coefs, dots = eye.astype(jnp.float32), gram
    for k in range(tasks):
        w = jnp.minimum(dots[k : k + 1, :], 0.0) * inverse[k : k + 1, :]
        w = jnp.broadcast_to(jnp.where(lane[:1] == k, 0.0, w), (tasks, LANES))
        coefs = coefs - jnp.where(sub == k, w, 0.0)
        dots = dots - columns[k] * w
    weight = jnp.sum(coefs, axis=1, keepdims=True)
    energy = jnp.sum(weight * jnp.sum(dots, axis=1, keepdims=True), axis=0, keepdims=True)
    rms = jnp.sqrt(jnp.maximum(energy, 0.0) / entries + EPS)
    weight = jnp.broadcast_to(weight * (0.5 / rms), (tasks, LANES))
    weights = [
        jnp.broadcast_to(jnp.sum(pick_ref[i] * weight, axis=0, keepdims=True), (GRAIN, LANES))
        for i in range(tasks)
    ]
    width = total_ref.shape[1]
    copies = []
    for row0, size, places_of in chunks:
        blocks = [(refs[k], base) for k, base in places_of]
        for top in range(0, size, OUT_ROWS):

            def body(r, _):
                at = pl.multiple_of(top + r * GRAIN, GRAIN)
                for c in range(0, width, LANES):
                    cols = pl.ds(c, LANES)
                    total = None
                    for i, weight in enumerate(weights):
                        block, base = blocks[i // per]
                        x = block[i % per, pl.ds(base + at, GRAIN), cols]
                        term = weight * x.astype(jnp.float32)
                        total = term if total is None else total + term
                    total_ref[pl.ds(row0 + at, GRAIN), cols] = total
                return 0

            lax.fori_loop(0, OUT_ROWS // GRAIN, body, 0)
            span = pl.ds(row0 + top, OUT_ROWS)
            copy = pltpu.make_async_copy(total_ref.at[span], out_ref.at[span], sems.at[len(copies)])
            copy.start()
            copies.append(copy)
    for copy in copies:
        copy.wait()


def combine(gram, tables_of, chunks, sizes, entries):
    blocks, layout, row0 = [], [], 0
    for chunk, size in zip(chunks, sizes):
        found = []
        for block, base in chunk:
            known = [k for k, b in enumerate(blocks) if b is block]
            if not known:
                blocks.append(block)
            found.append((known[0] if known else len(blocks) - 1, base))
        layout.append((row0, size, tuple(found)))
        row0 += size
    per, _, width = blocks[0].shape
    return pl.pallas_call(
        functools.partial(combine_kernel, per, entries, tuple(layout)),
        in_specs=[VMEM] * (1 + len(tables_of) + len(blocks)),
        out_specs=pl.BlockSpec(memory_space=pltpu.HBM),
        out_shape=jax.ShapeDtypeStruct((row0, width), jnp.float32),
        scratch_shapes=[
            pltpu.VMEM((row0, width), jnp.float32),
            pltpu.SemaphoreType.DMA((row0 // OUT_ROWS,)),
        ],
        compiler_params=pltpu.CompilerParams(vmem_limit_bytes=4 << 20),
        name="combine",
    )(gram, *tables_of, *blocks)


def cut_kernel(parts, pieces, grads_ref, *refs):
    outs, sems = refs[:-1], refs[-1]
    me = lax.axis_index("task")
    copies = []
    for k, (s, row0, size) in enumerate(pieces):
        block = outs[k].shape[-1]
        column = pl.multiple_of(lax.rem(me + s, parts) * block, block)
        source = grads_ref.at[:, pl.ds(row0, size), pl.ds(column, block)]
        copies.append(pltpu.make_async_copy(source, outs[k], sems.at[k]))
    for copy in copies:
        copy.start()
    for copy in copies:
        copy.wait()


def cut(grads, parts, pieces):
    per, _, width = grads.shape
    cuts = pl.pallas_call(
        functools.partial(cut_kernel, parts, pieces),
        in_specs=[pl.BlockSpec(memory_space=pltpu.HBM)],
        out_specs=[VMEM] * len(pieces),
        out_shape=[pltpu.VMEM((per, size, width // parts), grads.dtype) for _, _, size in pieces],
        scratch_shapes=[pltpu.SemaphoreType.DMA((len(pieces),))],
        compiler_params=pltpu.CompilerParams(vmem_limit_bytes=4 << 20),
        name="cut",
    )(pltpu.with_memory_space_constraint(grads, pltpu.HBM))
    return [near(c) for c in cuts]


def near(value):
    return pltpu.with_memory_space_constraint(value, pltpu.VMEM)


def shift(value, axis, by):
    n = lax.axis_size(axis)
    return near(lax.ppermute(value, axis, [(i, (i + by) % n) for i in range(n)]))


def shards(grads, order):
    per, rows, width = grads.shape
    parts, devices = lax.axis_size("task"), lax.axis_size(TASK_PARAM)
    entries = rows * lax.axis_size(PARAM) * width
    sent = {}
    for pieces in GROUPS:
        for piece, c in zip(pieces, cut(grads, parts, pieces)):
            sent[piece] = shift(c, "task", piece[0])
    own = cut(grads, parts, ((0, 0, rows),))[0]
    chunks, row0 = [], 0
    for size in CHUNKS:
        chunk = [(own, row0)]
        for s in SHIFTS:
            for (by, top, height), block in sent.items():
                if by == s and top <= row0 < top + height:
                    chunk.append((block, row0 - top))
        chunks.append(chunk)
        row0 += size
    gram, tables_of = None, None
    for k, (chunk, size) in enumerate(zip(chunks, CHUNKS)):
        gram, *more = gram_of(order, chunk, size, gram, devices, k == len(CHUNKS) - 1)
        tables_of = more or tables_of
    gram = lax.all_to_all(gram, TASK_PARAM, 0, 0, tiled=True)
    return combine(gram, tables_of, chunks, CHUNKS, entries)


def solution(mesh):
    torus = Mesh(
        mesh.devices.reshape(mesh.shape["task"], 4, 4, 2), ("task", "param_0", "param_1", "param_2")
    )
    in_specs = (P("task", PARAM, None), P())
    out_specs = P(PARAM, "task")
    return jax.shard_map(
        shards, mesh=torus, in_specs=in_specs, out_specs=out_specs, check_vma=False
    )
```

```python
import functools

import jax
import jax.numpy as jnp
from jax import lax
from jax.experimental import pallas as pl
from jax.experimental.pallas import tpu as pltpu
from jax.sharding import Mesh
from jax.sharding import PartitionSpec as P

PARAM = ("param_0", "param_1", "param_2")
TASK_PARAM = ("task", *PARAM)
CHUNKS = (192, 64)
SHIFTS = (2, 1, 3)
GROUPS = (((2, 0, 256), (1, 0, 192), (3, 0, 192)), ((1, 192, 64), (3, 192, 64)))
GRAIN = 16
OUT_ROWS = 64
LANES = 128
SUBLANES = 8
EPS = 1e-06
CANCEL = 0.001
VMEM = pl.BlockSpec(memory_space=pltpu.VMEM)
SMEM = pl.BlockSpec(memory_space=pltpu.SMEM)


def slot_tasks(parts, per):
    me = lax.axis_index("task")
    return [lax.rem(me + (parts - s), parts) * per + u for s in (0, *SHIFTS) for u in range(per)]


def tables(order_ref, slots, rows_ref, columns_ref, pick_ref):
    tasks = len(slots)

    def ordered(shape, dim):
        place, task = lax.broadcasted_iota(jnp.int32, shape, dim), jnp.full(shape, -1, jnp.int32)
        for k in range(tasks):
            task = jnp.where(place == k, order_ref[k], task)
        return task

    lane = lax.broadcasted_iota(jnp.int32, rows_ref.shape, 1)
    rows_ref[...] = jnp.where(lane // tasks == ordered(rows_ref.shape, 0), 1.0, 0.0)
    sub = lax.broadcasted_iota(jnp.int32, columns_ref.shape, 0)
    columns_ref[...] = jnp.where(sub % tasks == ordered(columns_ref.shape, 1), 1.0, 0.0)
    for i, task in enumerate(slots):
        pick_ref[i] = jnp.where(ordered(pick_ref.shape[1:], 0) == task, 1.0, 0.0)


def pieces_of(value):
    high = value.astype(jnp.bfloat16)
    rest = value - high.astype(jnp.float32)
    middle = rest.astype(jnp.bfloat16)
    return high, middle, (rest - middle.astype(jnp.float32)).astype(jnp.bfloat16)


def exact_dot(x, y, contract):
    return lax.dot_general(x, y, (contract, ((), ())), preferred_element_type=jnp.float32)


def gram_kernel(parts, per, rows, bases, first, last, *refs):
    if first:
        order_ref, refs = refs[0], refs[1:]
    blocks, refs = refs[:parts], refs[parts:]
    if not first:
        before_ref, refs = refs[0], refs[1:]
    out_ref, *refs = refs
    acc_ref = refs[-1] if last else out_ref
    tasks = parts * per
    width = blocks[0].shape[2]
    slots = slot_tasks(parts, per)
    pairs = [(i, j) for i in range(tasks) for j in range(i, tasks)]

    def body(r, sums):
        sums = list(sums)
        for c in range(width // LANES):
            cols = pl.ds(c * LANES, LANES)
            x = [
                b[u, pl.ds(base + r * GRAIN, GRAIN), cols].astype(jnp.float32)
                for b, base in zip(blocks, bases)
                for u in range(per)
            ]
            for h in range(GRAIN // SUBLANES):
                part = [v[h * SUBLANES : (h + 1) * SUBLANES] for v in x]
                for p, (i, j) in enumerate(pairs):
                    sums[p] = sums[p] + part[i] * part[j]
        return tuple(sums)

    zero = jnp.zeros((SUBLANES, LANES), jnp.float32)
    sums = lax.fori_loop(0, rows // GRAIN, body, (zero,) * len(pairs))
    square = tasks * tasks
    for p, (i, j) in enumerate(pairs):
        for a, b in ((i, j), (j, i))[: 1 if i == j else 2]:
            acc_ref[pl.ds(slots[a] * tasks + slots[b], SUBLANES, stride=square), :] = sums[p]
    if not first:
        acc_ref[...] += before_ref[...]
    if first:
        tables(order_ref, slots, *refs[:3])
    if last:
        folded = acc_ref[:square, :]
        for k in range(1, SUBLANES):
            folded = folded + acc_ref[k * square : (k + 1) * square, :]
        high, middle, low = pieces_of(folded)
        ones = jnp.ones((GRAIN, LANES), jnp.bfloat16)
        row = exact_dot(ones, jnp.concatenate([high, middle], axis=0), ((1,), (1,)))
        row += exact_dot(ones, jnp.concatenate([jnp.zeros_like(low), low], axis=0), ((1,), (1,)))
        out_ref[...] = jnp.broadcast_to(row[:1], out_ref.shape)


def gram_of(order, chunk, rows, before, devices, last):
    blocks, bases = zip(*chunk)
    parts, per = len(blocks), blocks[0].shape[0]
    tasks = parts * per
    table = (SUBLANES * tasks**2, LANES)
    first = before is None
    shapes = [(devices, LANES) if last else table]
    if first:
        shapes += [(tasks, LANES), (LANES, LANES), (tasks, tasks, LANES)]
    return pl.pallas_call(
        functools.partial(gram_kernel, parts, per, rows, bases, first, last),
        in_specs=[SMEM] * first + [VMEM] * (parts + (not first)),
        out_specs=[VMEM] * len(shapes),
        out_shape=[jax.ShapeDtypeStruct(shape, jnp.float32) for shape in shapes],
        scratch_shapes=[pltpu.VMEM(table, jnp.float32)] if last else [],
        compiler_params=pltpu.CompilerParams(vmem_limit_bytes=4 << 20),
        name="gram",
    )(*([order] if first else []), *blocks, *([] if first else [before]))


def combine_kernel(per, entries, chunks, gram_ref, rows_ref, columns_ref, pick_ref, *refs):
    refs, (out_ref, stats_ref, total_ref, sems) = refs[:-4], refs[-4:]
    tasks = rows_ref.shape[0]
    flat = jnp.sum(gram_ref[...], axis=0, keepdims=True)
    flat = flat + pltpu.roll(flat, tasks * tasks, 1)
    pieces = [p.astype(jnp.float32) for p in pieces_of(flat)]
    spread = jnp.concatenate([rows_ref[...] * p for p in pieces], axis=0).astype(jnp.bfloat16)
    found = exact_dot(spread, columns_ref[...].astype(jnp.bfloat16), ((1,), (0,)))
    gram = found[2 * tasks :] + found[tasks : 2 * tasks] + found[:tasks]
    lane = lax.broadcasted_iota(jnp.int32, (tasks, LANES), 1)
    sub = lax.broadcasted_iota(jnp.int32, (tasks, LANES), 0)
    eye = lane == sub
    norm = jnp.sum(jnp.where(eye, gram, 0.0), axis=1, keepdims=True)
    inverse = jnp.broadcast_to(1.0 / (norm + EPS), (tasks, LANES))
    columns = [jnp.broadcast_to(gram[:, k : k + 1], (tasks, LANES)) for k in range(tasks)]
    coefs, dots = eye.astype(jnp.float32), gram
    for k in range(tasks):
        w = jnp.minimum(dots[k : k + 1, :], 0.0) * inverse[k : k + 1, :]
        w = jnp.broadcast_to(jnp.where(lane[:1] == k, 0.0, w), (tasks, LANES))
        coefs = coefs - jnp.where(sub == k, w, 0.0)
        dots = dots - columns[k] * w
    weight = jnp.sum(coefs, axis=1, keepdims=True)
    energy = jnp.sum(weight * jnp.sum(dots, axis=1, keepdims=True), axis=0, keepdims=True)
    least = jnp.sum(jnp.abs(weight) * jnp.sqrt(jnp.maximum(norm, 0.0)), axis=0, keepdims=True)
    least = least * least * CANCEL
    scale = 0.5 / jnp.sqrt(jnp.maximum(energy, least) / entries + EPS)
    stats_ref[0] = jnp.max(least - energy)
    stats_ref[1] = jnp.max(scale)
    weight = jnp.broadcast_to(weight * scale, (tasks, LANES))
    weights = [
        jnp.broadcast_to(jnp.sum(pick_ref[i] * weight, axis=0, keepdims=True), (GRAIN, LANES))
        for i in range(tasks)
    ]
    width = total_ref.shape[1]
    copies = []
    for row0, size, places_of in chunks:
        blocks = [(refs[k], base) for k, base in places_of]
        for top in range(0, size, OUT_ROWS):

            def body(r, _):
                at = pl.multiple_of(top + r * GRAIN, GRAIN)
                for c in range(0, width, LANES):
                    cols = pl.ds(c, LANES)
                    total = None
                    for i, weight in enumerate(weights):
                        block, base = blocks[i // per]
                        x = block[i % per, pl.ds(base + at, GRAIN), cols]
                        term = weight * x.astype(jnp.float32)
                        total = term if total is None else total + term
                    total_ref[pl.ds(row0 + at, GRAIN), cols] = total
                return 0

            lax.fori_loop(0, OUT_ROWS // GRAIN, body, 0)
            span = pl.ds(row0 + top, OUT_ROWS)
            copy = pltpu.make_async_copy(total_ref.at[span], out_ref.at[span], sems.at[len(copies)])
            copy.start()
            copies.append(copy)
    for copy in copies:
        copy.wait()


def combine(gram, tables_of, chunks, sizes, entries):
    blocks, layout, row0 = [], [], 0
    for chunk, size in zip(chunks, sizes):
        found = []
        for block, base in chunk:
            known = [k for k, b in enumerate(blocks) if b is block]
            if not known:
                blocks.append(block)
            found.append((known[0] if known else len(blocks) - 1, base))
        layout.append((row0, size, tuple(found)))
        row0 += size
    per, _, width = blocks[0].shape
    return pl.pallas_call(
        functools.partial(combine_kernel, per, entries, tuple(layout)),
        in_specs=[VMEM] * (1 + len(tables_of) + len(blocks)),
        out_specs=[pl.BlockSpec(memory_space=pltpu.HBM), SMEM],
        out_shape=[
            pltpu.HBM((row0, width), jnp.float32),
            jax.ShapeDtypeStruct((2,), jnp.float32),
        ],
        scratch_shapes=[
            pltpu.VMEM((row0, width), jnp.float32),
            pltpu.SemaphoreType.DMA((row0 // OUT_ROWS,)),
        ],
        compiler_params=pltpu.CompilerParams(vmem_limit_bytes=4 << 20),
        name="combine",
    )(gram, *tables_of, *blocks)


def cut_kernel(parts, pieces, grads_ref, *refs):
    outs, sems = refs[:-1], refs[-1]
    me = lax.axis_index("task")
    copies = []
    for k, (s, row0, size) in enumerate(pieces):
        block = outs[k].shape[-1]
        column = pl.multiple_of(lax.rem(me + s, parts) * block, block)
        source = grads_ref.at[:, pl.ds(row0, size), pl.ds(column, block)]
        copies.append(pltpu.make_async_copy(source, outs[k], sems.at[k]))
    for copy in copies:
        copy.start()
    for copy in copies:
        copy.wait()


def cut(grads, parts, pieces):
    per, _, width = grads.shape
    cuts = pl.pallas_call(
        functools.partial(cut_kernel, parts, pieces),
        in_specs=[pl.BlockSpec(memory_space=pltpu.HBM)],
        out_specs=[VMEM] * len(pieces),
        out_shape=[pltpu.VMEM((per, size, width // parts), grads.dtype) for _, _, size in pieces],
        scratch_shapes=[pltpu.SemaphoreType.DMA((len(pieces),))],
        compiler_params=pltpu.CompilerParams(vmem_limit_bytes=4 << 20),
        name="cut",
    )(pltpu.with_memory_space_constraint(grads, pltpu.HBM))
    return [near(c) for c in cuts]


def near(value):
    return pltpu.with_memory_space_constraint(value, pltpu.VMEM)


def shift(value, axis, by):
    n = lax.axis_size(axis)
    return near(lax.ppermute(value, axis, [(i, (i + by) % n) for i in range(n)]))


def shards(grads, order):
    per, rows, width = grads.shape
    parts, devices = lax.axis_size("task"), lax.axis_size(TASK_PARAM)
    entries = rows * lax.axis_size(PARAM) * width
    sent = {}
    for pieces in GROUPS:
        for piece, c in zip(pieces, cut(grads, parts, pieces)):
            sent[piece] = shift(c, "task", piece[0])
    own = cut(grads, parts, ((0, 0, rows),))[0]
    chunks, row0 = [], 0
    for size in CHUNKS:
        chunk = [(own, row0)]
        for s in SHIFTS:
            for (by, top, height), block in sent.items():
                if by == s and top <= row0 < top + height:
                    chunk.append((block, row0 - top))
        chunks.append(chunk)
        row0 += size
    gram, tables_of = None, None
    for k, (chunk, size) in enumerate(zip(chunks, CHUNKS)):
        gram, *more = gram_of(order, chunk, size, gram, devices, k == len(CHUNKS) - 1)
        tables_of = more or tables_of
    gram = lax.all_to_all(gram, TASK_PARAM, 0, 0, tiled=True)
    update, stats = combine(gram, tables_of, chunks, CHUNKS, entries)

    def normalize(update):
        energy = functools.reduce(lax.psum, TASK_PARAM, jnp.sum(update * update))
        return update * (0.5 / jnp.sqrt(energy / entries + EPS * stats[1] * stats[1]))

    return lax.cond(stats[0] > 0.0, normalize, lambda update: update, update)


def solution(mesh):
    torus = Mesh(
        mesh.devices.reshape(mesh.shape["task"], 4, 4, 2), ("task", "param_0", "param_1", "param_2")
    )
    in_specs = (P("task", PARAM, None), P())
    out_specs = P(PARAM, "task")
    return jax.shard_map(
        shards, mesh=torus, in_specs=in_specs, out_specs=out_specs, check_vma=False
    )
```

```python
import functools

import jax
import jax.numpy as jnp
from jax import lax
from jax.experimental import pallas as pl
from jax.experimental.pallas import tpu as pltpu
from jax.sharding import Mesh
from jax.sharding import PartitionSpec as P

PARAM = ("param_0", "param_1", "param_2")
TASK_PARAM = ("task", *PARAM)
CHUNKS = (192, 64)
SHIFTS = (2, 1, 3)
GROUPS = (((2, 0, 256), (1, 0, 192), (3, 0, 192)), ((1, 192, 64), (3, 192, 64)))
GRAIN = 16
OUT_ROWS = 64
LANES = 128
SUBLANES = 8
EPS = 1e-06
CANCEL = 0.001
VMEM = pl.BlockSpec(memory_space=pltpu.VMEM)
SMEM = pl.BlockSpec(memory_space=pltpu.SMEM)


def slot_tasks(parts, per):
    me = lax.axis_index("task")
    return [lax.rem(me + (parts - s), parts) * per + u for s in (0, *SHIFTS) for u in range(per)]


def tables(order_ref, slots, rows_ref, columns_ref, pick_ref):
    tasks = len(slots)

    def ordered(shape, dim):
        place, task = lax.broadcasted_iota(jnp.int32, shape, dim), jnp.full(shape, -1, jnp.int32)
        for k in range(tasks):
            task = jnp.where(place == k, order_ref[k], task)
        return task

    lane = lax.broadcasted_iota(jnp.int32, rows_ref.shape, 1)
    rows_ref[...] = jnp.where(lane // tasks == ordered(rows_ref.shape, 0), 1.0, 0.0)
    sub = lax.broadcasted_iota(jnp.int32, columns_ref.shape, 0)
    columns_ref[...] = jnp.where(sub % tasks == ordered(columns_ref.shape, 1), 1.0, 0.0)
    for i, task in enumerate(slots):
        pick_ref[i] = jnp.where(ordered(pick_ref.shape[1:], 0) == task, 1.0, 0.0)


def pieces_of(value):
    high = value.astype(jnp.bfloat16)
    rest = value - high.astype(jnp.float32)
    middle = rest.astype(jnp.bfloat16)
    return high, middle, (rest - middle.astype(jnp.float32)).astype(jnp.bfloat16)


def exact_dot(x, y, contract):
    return lax.dot_general(x, y, (contract, ((), ())), preferred_element_type=jnp.float32)


def gram_kernel(parts, per, rows, bases, first, last, *refs):
    if first:
        order_ref, refs = refs[0], refs[1:]
    blocks, refs = refs[:parts], refs[parts:]
    if not first:
        before_ref, refs = refs[0], refs[1:]
    out_ref, *refs = refs
    acc_ref = refs[-1] if last else out_ref
    tasks = parts * per
    width = blocks[0].shape[2]
    slots = slot_tasks(parts, per)
    pairs = [(i, j) for i in range(tasks) for j in range(i, tasks)]

    def body(r, sums):
        sums = list(sums)
        for c in range(width // LANES):
            cols = pl.ds(c * LANES, LANES)
            x = [
                b[u, pl.ds(base + r * GRAIN, GRAIN), cols].astype(jnp.float32)
                for b, base in zip(blocks, bases)
                for u in range(per)
            ]
            for h in range(GRAIN // SUBLANES):
                part = [v[h * SUBLANES : (h + 1) * SUBLANES] for v in x]
                for p, (i, j) in enumerate(pairs):
                    sums[p] = sums[p] + part[i] * part[j]
        return tuple(sums)

    zero = jnp.zeros((SUBLANES, LANES), jnp.float32)
    sums = lax.fori_loop(0, rows // GRAIN, body, (zero,) * len(pairs))
    square = tasks * tasks
    for p, (i, j) in enumerate(pairs):
        for a, b in ((i, j), (j, i))[: 1 if i == j else 2]:
            acc_ref[pl.ds(slots[a] * tasks + slots[b], SUBLANES, stride=square), :] = sums[p]
    if not first:
        acc_ref[...] += before_ref[...]
    if first:
        tables(order_ref, slots, *refs[:3])
    if last:
        folded = acc_ref[:square, :]
        for k in range(1, SUBLANES):
            folded = folded + acc_ref[k * square : (k + 1) * square, :]
        high, middle, low = pieces_of(folded)
        ones = jnp.ones((GRAIN, LANES), jnp.bfloat16)
        row = exact_dot(ones, jnp.concatenate([high, middle], axis=0), ((1,), (1,)))
        row += exact_dot(ones, jnp.concatenate([jnp.zeros_like(low), low], axis=0), ((1,), (1,)))
        out_ref[...] = jnp.broadcast_to(row[:1], out_ref.shape)


def gram_of(order, chunk, rows, before, devices, last):
    blocks, bases = zip(*chunk)
    parts, per = len(blocks), blocks[0].shape[0]
    tasks = parts * per
    table = (SUBLANES * tasks**2, LANES)
    first = before is None
    shapes = [(devices, LANES) if last else table]
    if first:
        shapes += [(tasks, LANES), (LANES, LANES), (tasks, tasks, LANES)]
    return pl.pallas_call(
        functools.partial(gram_kernel, parts, per, rows, bases, first, last),
        in_specs=[SMEM] * first + [VMEM] * (parts + (not first)),
        out_specs=[VMEM] * len(shapes),
        out_shape=[jax.ShapeDtypeStruct(shape, jnp.float32) for shape in shapes],
        scratch_shapes=[pltpu.VMEM(table, jnp.float32)] if last else [],
        compiler_params=pltpu.CompilerParams(vmem_limit_bytes=4 << 20),
        name="gram",
    )(*([order] if first else []), *blocks, *([] if first else [before]))


def combine_kernel(per, entries, chunks, gram_ref, rows_ref, columns_ref, pick_ref, *refs):
    refs, (out_ref, poor_ref, scale_ref, total_ref, sems) = refs[:-5], refs[-5:]
    tasks = rows_ref.shape[0]
    flat = jnp.sum(gram_ref[...], axis=0, keepdims=True)
    flat = flat + pltpu.roll(flat, tasks * tasks, 1)
    pieces = [p.astype(jnp.float32) for p in pieces_of(flat)]
    spread = jnp.concatenate([rows_ref[...] * p for p in pieces], axis=0).astype(jnp.bfloat16)
    found = exact_dot(spread, columns_ref[...].astype(jnp.bfloat16), ((1,), (0,)))
    gram = found[2 * tasks :] + found[tasks : 2 * tasks] + found[:tasks]
    lane = lax.broadcasted_iota(jnp.int32, (tasks, LANES), 1)
    sub = lax.broadcasted_iota(jnp.int32, (tasks, LANES), 0)
    eye = lane == sub
    norm = jnp.sum(jnp.where(eye, gram, 0.0), axis=1, keepdims=True)
    inverse = jnp.broadcast_to(1.0 / (norm + EPS), (tasks, LANES))
    columns = [jnp.broadcast_to(gram[:, k : k + 1], (tasks, LANES)) for k in range(tasks)]
    coefs, dots = eye.astype(jnp.float32), gram
    for k in range(tasks):
        w = jnp.minimum(dots[k : k + 1, :], 0.0) * inverse[k : k + 1, :]
        w = jnp.broadcast_to(jnp.where(lane[:1] == k, 0.0, w), (tasks, LANES))
        coefs = coefs - jnp.where(sub == k, w, 0.0)
        dots = dots - columns[k] * w
    weight = jnp.sum(coefs, axis=1, keepdims=True)
    energy = jnp.sum(weight * jnp.sum(dots, axis=1, keepdims=True), axis=0, keepdims=True)
    least = jnp.sum(jnp.abs(weight) * jnp.sqrt(jnp.maximum(norm, 0.0)), axis=0, keepdims=True)
    least = least * least * CANCEL
    scale = 0.5 / jnp.sqrt(jnp.maximum(energy, least) / entries + EPS)
    poor_ref[...] = jnp.broadcast_to(least - energy, (1, LANES)).reshape(LANES)
    scale_ref[...] = jnp.broadcast_to(scale, (1, LANES)).reshape(LANES)
    weight = jnp.broadcast_to(weight * scale, (tasks, LANES))
    weights = [
        jnp.broadcast_to(jnp.sum(pick_ref[i] * weight, axis=0, keepdims=True), (GRAIN, LANES))
        for i in range(tasks)
    ]
    width = total_ref.shape[1]
    copies = []
    for row0, size, places_of in chunks:
        blocks = [(refs[k], base) for k, base in places_of]
        for top in range(0, size, OUT_ROWS):

            def body(r, _):
                at = pl.multiple_of(top + r * GRAIN, GRAIN)
                for c in range(0, width, LANES):
                    cols = pl.ds(c, LANES)
                    total = None
                    for i, weight in enumerate(weights):
                        block, base = blocks[i // per]
                        x = block[i % per, pl.ds(base + at, GRAIN), cols]
                        term = weight * x.astype(jnp.float32)
                        total = term if total is None else total + term
                    total_ref[pl.ds(row0 + at, GRAIN), cols] = total
                return 0

            lax.fori_loop(0, OUT_ROWS // GRAIN, body, 0)
            span = pl.ds(row0 + top, OUT_ROWS)
            copy = pltpu.make_async_copy(total_ref.at[span], out_ref.at[span], sems.at[len(copies)])
            copy.start()
            copies.append(copy)
    for copy in copies:
        copy.wait()


def combine(gram, tables_of, chunks, sizes, entries):
    blocks, layout, row0 = [], [], 0
    for chunk, size in zip(chunks, sizes):
        found = []
        for block, base in chunk:
            known = [k for k, b in enumerate(blocks) if b is block]
            if not known:
                blocks.append(block)
            found.append((known[0] if known else len(blocks) - 1, base))
        layout.append((row0, size, tuple(found)))
        row0 += size
    per, _, width = blocks[0].shape
    return pl.pallas_call(
        functools.partial(combine_kernel, per, entries, tuple(layout)),
        in_specs=[VMEM] * (1 + len(tables_of) + len(blocks)),
        out_specs=[pl.BlockSpec(memory_space=pltpu.HBM), VMEM, VMEM],
        out_shape=[
            pltpu.HBM((row0, width), jnp.float32),
            jax.ShapeDtypeStruct((LANES,), jnp.float32),
            jax.ShapeDtypeStruct((LANES,), jnp.float32),
        ],
        scratch_shapes=[
            pltpu.VMEM((row0, width), jnp.float32),
            pltpu.SemaphoreType.DMA((row0 // OUT_ROWS,)),
        ],
        compiler_params=pltpu.CompilerParams(vmem_limit_bytes=4 << 20),
        name="combine",
    )(gram, *tables_of, *blocks)


def cut_kernel(parts, pieces, grads_ref, *refs):
    outs, sems = refs[:-1], refs[-1]
    me = lax.axis_index("task")
    copies = []
    for k, (s, row0, size) in enumerate(pieces):
        block = outs[k].shape[-1]
        column = pl.multiple_of(lax.rem(me + s, parts) * block, block)
        source = grads_ref.at[:, pl.ds(row0, size), pl.ds(column, block)]
        copies.append(pltpu.make_async_copy(source, outs[k], sems.at[k]))
    for copy in copies:
        copy.start()
    for copy in copies:
        copy.wait()


def cut(grads, parts, pieces):
    per, _, width = grads.shape
    cuts = pl.pallas_call(
        functools.partial(cut_kernel, parts, pieces),
        in_specs=[pl.BlockSpec(memory_space=pltpu.HBM)],
        out_specs=[VMEM] * len(pieces),
        out_shape=[pltpu.VMEM((per, size, width // parts), grads.dtype) for _, _, size in pieces],
        scratch_shapes=[pltpu.SemaphoreType.DMA((len(pieces),))],
        compiler_params=pltpu.CompilerParams(vmem_limit_bytes=4 << 20),
        name="cut",
    )(pltpu.with_memory_space_constraint(grads, pltpu.HBM))
    return [near(c) for c in cuts]


def near(value):
    return pltpu.with_memory_space_constraint(value, pltpu.VMEM)


def shift(value, axis, by):
    n = lax.axis_size(axis)
    return near(lax.ppermute(value, axis, [(i, (i + by) % n) for i in range(n)]))


def shards(grads, order):
    per, rows, width = grads.shape
    parts, devices = lax.axis_size("task"), lax.axis_size(TASK_PARAM)
    entries = rows * lax.axis_size(PARAM) * width
    sent = {}
    for pieces in GROUPS:
        for piece, c in zip(pieces, cut(grads, parts, pieces)):
            sent[piece] = shift(c, "task", piece[0])
    own = cut(grads, parts, ((0, 0, rows),))[0]
    chunks, row0 = [], 0
    for size in CHUNKS:
        chunk = [(own, row0)]
        for s in SHIFTS:
            for (by, top, height), block in sent.items():
                if by == s and top <= row0 < top + height:
                    chunk.append((block, row0 - top))
        chunks.append(chunk)
        row0 += size
    gram, tables_of = None, None
    for k, (chunk, size) in enumerate(zip(chunks, CHUNKS)):
        gram, *more = gram_of(order, chunk, size, gram, devices, k == len(CHUNKS) - 1)
        tables_of = more or tables_of
    gram = lax.all_to_all(gram, TASK_PARAM, 0, 0, tiled=True)
    update, poor, scale = combine(gram, tables_of, chunks, CHUNKS, entries)

    def normalize(update):
        energy = functools.reduce(lax.psum, TASK_PARAM, jnp.sum(update * update))
        return update * (0.5 / jnp.sqrt(energy / entries + EPS * scale[0] * scale[0]))

    return lax.cond(poor[0] > 0.0, normalize, lambda update: update, update)


def solution(mesh):
    torus = Mesh(
        mesh.devices.reshape(mesh.shape["task"], 4, 4, 2), ("task", "param_0", "param_1", "param_2")
    )
    in_specs = (P("task", PARAM, None), P())
    out_specs = P(PARAM, "task")
    return jax.shard_map(
        shards, mesh=torus, in_specs=in_specs, out_specs=out_specs, check_vma=False
    )
```

```python
import functools

import jax
import jax.numpy as jnp
from jax import lax
from jax.experimental import pallas as pl
from jax.experimental.pallas import tpu as pltpu
from jax.sharding import Mesh
from jax.sharding import PartitionSpec as P

PARAM = ("param_0", "param_1", "param_2")
TASK_PARAM = ("task", *PARAM)
CHUNKS = (192, 64)
SHIFTS = (2, 1, 3)
GROUPS = (((2, 0, 256),), ((1, 0, 192), (3, 0, 192)), ((1, 192, 64), (3, 192, 64)))
GRAIN = 16
OUT_ROWS = 64
LANES = 128
SUBLANES = 8
EPS = 1e-06
CANCEL = 0.001
VMEM = pl.BlockSpec(memory_space=pltpu.VMEM)
SMEM = pl.BlockSpec(memory_space=pltpu.SMEM)


def slot_tasks(parts, per):
    me = lax.axis_index("task")
    return [lax.rem(me + (parts - s), parts) * per + u for s in (0, *SHIFTS) for u in range(per)]


def tables(order_ref, slots, rows_ref, columns_ref, pick_ref):
    tasks = len(slots)

    def ordered(shape, dim):
        place, task = lax.broadcasted_iota(jnp.int32, shape, dim), jnp.full(shape, -1, jnp.int32)
        for k in range(tasks):
            task = jnp.where(place == k, order_ref[k], task)
        return task

    lane = lax.broadcasted_iota(jnp.int32, rows_ref.shape, 1)
    rows_ref[...] = jnp.where(lane // tasks == ordered(rows_ref.shape, 0), 1.0, 0.0)
    sub = lax.broadcasted_iota(jnp.int32, columns_ref.shape, 0)
    columns_ref[...] = jnp.where(sub % tasks == ordered(columns_ref.shape, 1), 1.0, 0.0)
    for i, task in enumerate(slots):
        pick_ref[i] = jnp.where(ordered(pick_ref.shape[1:], 0) == task, 1.0, 0.0)


def pieces_of(value):
    high = value.astype(jnp.bfloat16)
    rest = value - high.astype(jnp.float32)
    middle = rest.astype(jnp.bfloat16)
    return high, middle, (rest - middle.astype(jnp.float32)).astype(jnp.bfloat16)


def exact_dot(x, y, contract):
    return lax.dot_general(x, y, (contract, ((), ())), preferred_element_type=jnp.float32)


def gram_kernel(parts, per, rows, bases, first, last, *refs):
    if first:
        order_ref, refs = refs[0], refs[1:]
    blocks, refs = refs[:parts], refs[parts:]
    if not first:
        before_ref, refs = refs[0], refs[1:]
    out_ref, *refs = refs
    acc_ref = refs[-1] if last else out_ref
    tasks = parts * per
    width = blocks[0].shape[2]
    slots = slot_tasks(parts, per)
    pairs = [(i, j) for i in range(tasks) for j in range(i, tasks)]

    def body(r, sums):
        sums = list(sums)
        for c in range(width // LANES):
            cols = pl.ds(c * LANES, LANES)
            x = [
                b[u, pl.ds(base + r * GRAIN, GRAIN), cols].astype(jnp.float32)
                for b, base in zip(blocks, bases)
                for u in range(per)
            ]
            for h in range(GRAIN // SUBLANES):
                part = [v[h * SUBLANES : (h + 1) * SUBLANES] for v in x]
                for p, (i, j) in enumerate(pairs):
                    sums[p] = sums[p] + part[i] * part[j]
        return tuple(sums)

    zero = jnp.zeros((SUBLANES, LANES), jnp.float32)
    sums = lax.fori_loop(0, rows // GRAIN, body, (zero,) * len(pairs))
    square = tasks * tasks
    for p, (i, j) in enumerate(pairs):
        for a, b in ((i, j), (j, i))[: 1 if i == j else 2]:
            acc_ref[pl.ds(slots[a] * tasks + slots[b], SUBLANES, stride=square), :] = sums[p]
    if not first:
        acc_ref[...] += before_ref[...]
    if first:
        tables(order_ref, slots, *refs[:3])
    if last:
        folded = acc_ref[:square, :]
        for k in range(1, SUBLANES):
            folded = folded + acc_ref[k * square : (k + 1) * square, :]
        high, middle, low = pieces_of(folded)
        ones = jnp.ones((GRAIN, LANES), jnp.bfloat16)
        row = exact_dot(ones, jnp.concatenate([high, middle], axis=0), ((1,), (1,)))
        row += exact_dot(ones, jnp.concatenate([jnp.zeros_like(low), low], axis=0), ((1,), (1,)))
        out_ref[...] = jnp.broadcast_to(row[:1], out_ref.shape)


def gram_of(order, chunk, rows, before, devices, last):
    blocks, bases = zip(*chunk)
    parts, per = len(blocks), blocks[0].shape[0]
    tasks = parts * per
    table = (SUBLANES * tasks**2, LANES)
    first = before is None
    shapes = [(devices, LANES) if last else table]
    if first:
        shapes += [(tasks, LANES), (LANES, LANES), (tasks, tasks, LANES)]
    return pl.pallas_call(
        functools.partial(gram_kernel, parts, per, rows, bases, first, last),
        in_specs=[SMEM] * first + [VMEM] * (parts + (not first)),
        out_specs=[VMEM] * len(shapes),
        out_shape=[jax.ShapeDtypeStruct(shape, jnp.float32) for shape in shapes],
        scratch_shapes=[pltpu.VMEM(table, jnp.float32)] if last else [],
        compiler_params=pltpu.CompilerParams(vmem_limit_bytes=4 << 20),
        name="gram",
    )(*([order] if first else []), *blocks, *([] if first else [before]))


def combine_kernel(per, entries, chunks, gram_ref, rows_ref, columns_ref, pick_ref, *refs):
    refs, (out_ref, poor_ref, scale_ref, total_ref, sems) = refs[:-5], refs[-5:]
    tasks = rows_ref.shape[0]
    flat = jnp.sum(gram_ref[...], axis=0, keepdims=True)
    flat = flat + pltpu.roll(flat, tasks * tasks, 1)
    pieces = [p.astype(jnp.float32) for p in pieces_of(flat)]
    spread = jnp.concatenate([rows_ref[...] * p for p in pieces], axis=0).astype(jnp.bfloat16)
    found = exact_dot(spread, columns_ref[...].astype(jnp.bfloat16), ((1,), (0,)))
    gram = found[2 * tasks :] + found[tasks : 2 * tasks] + found[:tasks]
    lane = lax.broadcasted_iota(jnp.int32, (tasks, LANES), 1)
    sub = lax.broadcasted_iota(jnp.int32, (tasks, LANES), 0)
    eye = lane == sub
    norm = jnp.sum(jnp.where(eye, gram, 0.0), axis=1, keepdims=True)
    inverse = jnp.broadcast_to(1.0 / (norm + EPS), (tasks, LANES))
    columns = [jnp.broadcast_to(gram[:, k : k + 1], (tasks, LANES)) for k in range(tasks)]
    coefs, dots = eye.astype(jnp.float32), gram
    for k in range(tasks):
        w = jnp.minimum(dots[k : k + 1, :], 0.0) * inverse[k : k + 1, :]
        w = jnp.broadcast_to(jnp.where(lane[:1] == k, 0.0, w), (tasks, LANES))
        coefs = coefs - jnp.where(sub == k, w, 0.0)
        dots = dots - columns[k] * w
    weight = jnp.sum(coefs, axis=1, keepdims=True)
    energy = jnp.sum(weight * jnp.sum(dots, axis=1, keepdims=True), axis=0, keepdims=True)
    least = jnp.sum(jnp.abs(weight) * jnp.sqrt(jnp.maximum(norm, 0.0)), axis=0, keepdims=True)
    least = least * least * CANCEL
    scale = 0.5 / jnp.sqrt(jnp.maximum(energy, least) / entries + EPS)
    poor_ref[...] = jnp.broadcast_to(least - energy, (1, LANES)).reshape(LANES)
    scale_ref[...] = jnp.broadcast_to(scale, (1, LANES)).reshape(LANES)
    weight = jnp.broadcast_to(weight * scale, (tasks, LANES))
    weights = [
        jnp.broadcast_to(jnp.sum(pick_ref[i] * weight, axis=0, keepdims=True), (GRAIN, LANES))
        for i in range(tasks)
    ]
    width = total_ref.shape[1]
    copies = []
    for row0, size, places_of in chunks:
        blocks = [(refs[k], base) for k, base in places_of]
        for top in range(0, size, OUT_ROWS):

            def body(r, _):
                at = pl.multiple_of(top + r * GRAIN, GRAIN)
                for c in range(0, width, LANES):
                    cols = pl.ds(c, LANES)
                    total = None
                    for i, weight in enumerate(weights):
                        block, base = blocks[i // per]
                        x = block[i % per, pl.ds(base + at, GRAIN), cols]
                        term = weight * x.astype(jnp.float32)
                        total = term if total is None else total + term
                    total_ref[pl.ds(row0 + at, GRAIN), cols] = total
                return 0

            lax.fori_loop(0, OUT_ROWS // GRAIN, body, 0)
            span = pl.ds(row0 + top, OUT_ROWS)
            copy = pltpu.make_async_copy(total_ref.at[span], out_ref.at[span], sems.at[len(copies)])
            copy.start()
            copies.append(copy)
    for copy in copies:
        copy.wait()


def combine(gram, tables_of, chunks, sizes, entries):
    blocks, layout, row0 = [], [], 0
    for chunk, size in zip(chunks, sizes):
        found = []
        for block, base in chunk:
            known = [k for k, b in enumerate(blocks) if b is block]
            if not known:
                blocks.append(block)
            found.append((known[0] if known else len(blocks) - 1, base))
        layout.append((row0, size, tuple(found)))
        row0 += size
    per, _, width = blocks[0].shape
    return pl.pallas_call(
        functools.partial(combine_kernel, per, entries, tuple(layout)),
        in_specs=[VMEM] * (1 + len(tables_of) + len(blocks)),
        out_specs=[pl.BlockSpec(memory_space=pltpu.HBM), VMEM, VMEM],
        out_shape=[
            pltpu.HBM((row0, width), jnp.float32),
            jax.ShapeDtypeStruct((LANES,), jnp.float32),
            jax.ShapeDtypeStruct((LANES,), jnp.float32),
        ],
        scratch_shapes=[
            pltpu.VMEM((row0, width), jnp.float32),
            pltpu.SemaphoreType.DMA((row0 // OUT_ROWS,)),
        ],
        compiler_params=pltpu.CompilerParams(vmem_limit_bytes=4 << 20),
        name="combine",
    )(gram, *tables_of, *blocks)


def cut_kernel(parts, pieces, grads_ref, *refs):
    outs, sems = refs[:-1], refs[-1]
    me = lax.axis_index("task")
    copies = []
    for k, (s, row0, size) in enumerate(pieces):
        block = outs[k].shape[-1]
        column = pl.multiple_of(lax.rem(me + s, parts) * block, block)
        source = grads_ref.at[:, pl.ds(row0, size), pl.ds(column, block)]
        copies.append(pltpu.make_async_copy(source, outs[k], sems.at[k]))
    for copy in copies:
        copy.start()
    for copy in copies:
        copy.wait()


def cut(grads, parts, pieces):
    per, _, width = grads.shape
    cuts = pl.pallas_call(
        functools.partial(cut_kernel, parts, pieces),
        in_specs=[pl.BlockSpec(memory_space=pltpu.HBM)],
        out_specs=[VMEM] * len(pieces),
        out_shape=[pltpu.VMEM((per, size, width // parts), grads.dtype) for _, _, size in pieces],
        scratch_shapes=[pltpu.SemaphoreType.DMA((len(pieces),))],
        compiler_params=pltpu.CompilerParams(vmem_limit_bytes=4 << 20),
        name="cut",
    )(pltpu.with_memory_space_constraint(grads, pltpu.HBM))
    return [near(c) for c in cuts]


def near(value):
    return pltpu.with_memory_space_constraint(value, pltpu.VMEM)


def shift(value, axis, by):
    n = lax.axis_size(axis)
    return near(lax.ppermute(value, axis, [(i, (i + by) % n) for i in range(n)]))


def shards(grads, order):
    per, rows, width = grads.shape
    parts, devices = lax.axis_size("task"), lax.axis_size(TASK_PARAM)
    entries = rows * lax.axis_size(PARAM) * width
    sent = {}
    for pieces in GROUPS:
        for piece, c in zip(pieces, cut(grads, parts, pieces)):
            sent[piece] = shift(c, "task", piece[0])
    own = cut(grads, parts, ((0, 0, rows),))[0]
    chunks, row0 = [], 0
    for size in CHUNKS:
        chunk = [(own, row0)]
        for s in SHIFTS:
            for (by, top, height), block in sent.items():
                if by == s and top <= row0 < top + height:
                    chunk.append((block, row0 - top))
        chunks.append(chunk)
        row0 += size
    gram, tables_of = None, None
    for k, (chunk, size) in enumerate(zip(chunks, CHUNKS)):
        gram, *more = gram_of(order, chunk, size, gram, devices, k == len(CHUNKS) - 1)
        tables_of = more or tables_of
    gram = lax.all_to_all(gram, TASK_PARAM, 0, 0, tiled=True)
    update, poor, scale = combine(gram, tables_of, chunks, CHUNKS, entries)

    def normalize(update):
        energy = functools.reduce(lax.psum, TASK_PARAM, jnp.sum(update * update))
        return update * (0.5 / jnp.sqrt(energy / entries + EPS * scale[0] * scale[0]))

    return lax.cond(poor[0] > 0.0, normalize, lambda update: update, update)


def solution(mesh):
    torus = Mesh(
        mesh.devices.reshape(mesh.shape["task"], 4, 4, 2), ("task", "param_0", "param_1", "param_2")
    )
    in_specs = (P("task", PARAM, None), P())
    out_specs = P(PARAM, "task")
    return jax.shard_map(
        shards, mesh=torus, in_specs=in_specs, out_specs=out_specs, check_vma=False
    )
```

```python
import functools

import jax
import jax.numpy as jnp
from jax import lax
from jax.experimental import pallas as pl
from jax.experimental.pallas import tpu as pltpu
from jax.sharding import Mesh
from jax.sharding import PartitionSpec as P

PARAM = ("param_0", "param_1", "param_2")
TASK_PARAM = ("task", *PARAM)
CHUNKS = (208, 48)
SHIFTS = (2, 1, 3)
GROUPS = (((2, 0, 256), (1, 0, 208), (3, 0, 208)), ((1, 208, 48), (3, 208, 48)))
GRAIN = 16
OUT_ROWS = 64
LANES = 128
SUBLANES = 8
EPS = 1e-06
CANCEL = 0.001
VMEM = pl.BlockSpec(memory_space=pltpu.VMEM)
SMEM = pl.BlockSpec(memory_space=pltpu.SMEM)


def slot_tasks(parts, per):
    me = lax.axis_index("task")
    return [lax.rem(me + (parts - s), parts) * per + u for s in (0, *SHIFTS) for u in range(per)]


def tables(order_ref, slots, rows_ref, columns_ref, pick_ref):
    tasks = len(slots)

    def ordered(shape, dim):
        place, task = lax.broadcasted_iota(jnp.int32, shape, dim), jnp.full(shape, -1, jnp.int32)
        for k in range(tasks):
            task = jnp.where(place == k, order_ref[k], task)
        return task

    lane = lax.broadcasted_iota(jnp.int32, rows_ref.shape, 1)
    rows_ref[...] = jnp.where(lane // tasks == ordered(rows_ref.shape, 0), 1.0, 0.0)
    sub = lax.broadcasted_iota(jnp.int32, columns_ref.shape, 0)
    columns_ref[...] = jnp.where(sub % tasks == ordered(columns_ref.shape, 1), 1.0, 0.0)
    for i, task in enumerate(slots):
        pick_ref[i] = jnp.where(ordered(pick_ref.shape[1:], 0) == task, 1.0, 0.0)


def pieces_of(value):
    high = value.astype(jnp.bfloat16)
    rest = value - high.astype(jnp.float32)
    middle = rest.astype(jnp.bfloat16)
    return high, middle, (rest - middle.astype(jnp.float32)).astype(jnp.bfloat16)


def exact_dot(x, y, contract):
    return lax.dot_general(x, y, (contract, ((), ())), preferred_element_type=jnp.float32)


def gram_kernel(parts, per, rows, bases, first, last, *refs):
    if first:
        order_ref, refs = refs[0], refs[1:]
    blocks, refs = refs[:parts], refs[parts:]
    if not first:
        before_ref, refs = refs[0], refs[1:]
    out_ref, *refs = refs
    acc_ref = refs[-1] if last else out_ref
    tasks = parts * per
    width = blocks[0].shape[2]
    slots = slot_tasks(parts, per)
    pairs = [(i, j) for i in range(tasks) for j in range(i, tasks)]

    def body(r, sums):
        sums = list(sums)
        for c in range(width // LANES):
            cols = pl.ds(c * LANES, LANES)
            x = [
                b[u, pl.ds(base + r * GRAIN, GRAIN), cols].astype(jnp.float32)
                for b, base in zip(blocks, bases)
                for u in range(per)
            ]
            for h in range(GRAIN // SUBLANES):
                part = [v[h * SUBLANES : (h + 1) * SUBLANES] for v in x]
                for p, (i, j) in enumerate(pairs):
                    sums[p] = sums[p] + part[i] * part[j]
        return tuple(sums)

    zero = jnp.zeros((SUBLANES, LANES), jnp.float32)
    sums = lax.fori_loop(0, rows // GRAIN, body, (zero,) * len(pairs))
    square = tasks * tasks
    for p, (i, j) in enumerate(pairs):
        for a, b in ((i, j), (j, i))[: 1 if i == j else 2]:
            acc_ref[pl.ds(slots[a] * tasks + slots[b], SUBLANES, stride=square), :] = sums[p]
    if not first:
        acc_ref[...] += before_ref[...]
    if first:
        tables(order_ref, slots, *refs[:3])
    if last:
        folded = acc_ref[:square, :]
        for k in range(1, SUBLANES):
            folded = folded + acc_ref[k * square : (k + 1) * square, :]
        high, middle, low = pieces_of(folded)
        ones = jnp.ones((GRAIN, LANES), jnp.bfloat16)
        row = exact_dot(ones, jnp.concatenate([high, middle], axis=0), ((1,), (1,)))
        row += exact_dot(ones, jnp.concatenate([jnp.zeros_like(low), low], axis=0), ((1,), (1,)))
        out_ref[...] = jnp.broadcast_to(row[:1], out_ref.shape)


def gram_of(order, chunk, rows, before, devices, last):
    blocks, bases = zip(*chunk)
    parts, per = len(blocks), blocks[0].shape[0]
    tasks = parts * per
    table = (SUBLANES * tasks**2, LANES)
    first = before is None
    shapes = [(devices, LANES) if last else table]
    if first:
        shapes += [(tasks, LANES), (LANES, LANES), (tasks, tasks, LANES)]
    return pl.pallas_call(
        functools.partial(gram_kernel, parts, per, rows, bases, first, last),
        in_specs=[SMEM] * first + [VMEM] * (parts + (not first)),
        out_specs=[VMEM] * len(shapes),
        out_shape=[jax.ShapeDtypeStruct(shape, jnp.float32) for shape in shapes],
        scratch_shapes=[pltpu.VMEM(table, jnp.float32)] if last else [],
        compiler_params=pltpu.CompilerParams(vmem_limit_bytes=4 << 20),
        name="gram",
    )(*([order] if first else []), *blocks, *([] if first else [before]))


def combine_kernel(per, entries, chunks, gram_ref, rows_ref, columns_ref, pick_ref, *refs):
    refs, (out_ref, poor_ref, scale_ref, total_ref, sems) = refs[:-5], refs[-5:]
    tasks = rows_ref.shape[0]
    flat = jnp.sum(gram_ref[...], axis=0, keepdims=True)
    flat = flat + pltpu.roll(flat, tasks * tasks, 1)
    pieces = [p.astype(jnp.float32) for p in pieces_of(flat)]
    spread = jnp.concatenate([rows_ref[...] * p for p in pieces], axis=0).astype(jnp.bfloat16)
    found = exact_dot(spread, columns_ref[...].astype(jnp.bfloat16), ((1,), (0,)))
    gram = found[2 * tasks :] + found[tasks : 2 * tasks] + found[:tasks]
    lane = lax.broadcasted_iota(jnp.int32, (tasks, LANES), 1)
    sub = lax.broadcasted_iota(jnp.int32, (tasks, LANES), 0)
    eye = lane == sub
    norm = jnp.sum(jnp.where(eye, gram, 0.0), axis=1, keepdims=True)
    inverse = jnp.broadcast_to(1.0 / (norm + EPS), (tasks, LANES))
    columns = [jnp.broadcast_to(gram[:, k : k + 1], (tasks, LANES)) for k in range(tasks)]
    coefs, dots = eye.astype(jnp.float32), gram
    for k in range(tasks):
        w = jnp.minimum(dots[k : k + 1, :], 0.0) * inverse[k : k + 1, :]
        w = jnp.broadcast_to(jnp.where(lane[:1] == k, 0.0, w), (tasks, LANES))
        coefs = coefs - jnp.where(sub == k, w, 0.0)
        dots = dots - columns[k] * w
    weight = jnp.sum(coefs, axis=1, keepdims=True)
    energy = jnp.sum(weight * jnp.sum(dots, axis=1, keepdims=True), axis=0, keepdims=True)
    least = jnp.sum(jnp.abs(weight) * jnp.sqrt(jnp.maximum(norm, 0.0)), axis=0, keepdims=True)
    least = least * least * CANCEL
    scale = 0.5 / jnp.sqrt(jnp.maximum(energy, least) / entries + EPS)
    poor_ref[...] = jnp.broadcast_to(least - energy, (1, LANES)).reshape(LANES)
    scale_ref[...] = jnp.broadcast_to(scale, (1, LANES)).reshape(LANES)
    weight = jnp.broadcast_to(weight * scale, (tasks, LANES))
    weights = [
        jnp.broadcast_to(jnp.sum(pick_ref[i] * weight, axis=0, keepdims=True), (GRAIN, LANES))
        for i in range(tasks)
    ]
    width = total_ref.shape[1]
    copies = []
    for row0, size, places_of in chunks:
        blocks = [(refs[k], base) for k, base in places_of]
        for top in range(0, size, OUT_ROWS):
            here = min(OUT_ROWS, size - top)

            def body(r, _):
                at = pl.multiple_of(top + r * GRAIN, GRAIN)
                for c in range(0, width, LANES):
                    cols = pl.ds(c, LANES)
                    total = None
                    for i, weight in enumerate(weights):
                        block, base = blocks[i // per]
                        x = block[i % per, pl.ds(base + at, GRAIN), cols]
                        term = weight * x.astype(jnp.float32)
                        total = term if total is None else total + term
                    total_ref[pl.ds(row0 + at, GRAIN), cols] = total
                return 0

            lax.fori_loop(0, here // GRAIN, body, 0)
            span = pl.ds(row0 + top, here)
            copy = pltpu.make_async_copy(total_ref.at[span], out_ref.at[span], sems.at[len(copies)])
            copy.start()
            copies.append(copy)
    for copy in copies:
        copy.wait()


def combine(gram, tables_of, chunks, sizes, entries):
    blocks, layout, row0 = [], [], 0
    for chunk, size in zip(chunks, sizes):
        found = []
        for block, base in chunk:
            known = [k for k, b in enumerate(blocks) if b is block]
            if not known:
                blocks.append(block)
            found.append((known[0] if known else len(blocks) - 1, base))
        layout.append((row0, size, tuple(found)))
        row0 += size
    per, _, width = blocks[0].shape
    return pl.pallas_call(
        functools.partial(combine_kernel, per, entries, tuple(layout)),
        in_specs=[VMEM] * (1 + len(tables_of) + len(blocks)),
        out_specs=[pl.BlockSpec(memory_space=pltpu.HBM), VMEM, VMEM],
        out_shape=[
            pltpu.HBM((row0, width), jnp.float32),
            jax.ShapeDtypeStruct((LANES,), jnp.float32),
            jax.ShapeDtypeStruct((LANES,), jnp.float32),
        ],
        scratch_shapes=[
            pltpu.VMEM((row0, width), jnp.float32),
            pltpu.SemaphoreType.DMA((sum(-(-size // OUT_ROWS) for size in sizes),)),
        ],
        compiler_params=pltpu.CompilerParams(vmem_limit_bytes=4 << 20),
        name="combine",
    )(gram, *tables_of, *blocks)


def cut_kernel(parts, pieces, grads_ref, *refs):
    outs, sems = refs[:-1], refs[-1]
    me = lax.axis_index("task")
    copies = []
    for k, (s, row0, size) in enumerate(pieces):
        block = outs[k].shape[-1]
        column = pl.multiple_of(lax.rem(me + s, parts) * block, block)
        source = grads_ref.at[:, pl.ds(row0, size), pl.ds(column, block)]
        copies.append(pltpu.make_async_copy(source, outs[k], sems.at[k]))
    for copy in copies:
        copy.start()
    for copy in copies:
        copy.wait()


def cut(grads, parts, pieces):
    per, _, width = grads.shape
    cuts = pl.pallas_call(
        functools.partial(cut_kernel, parts, pieces),
        in_specs=[pl.BlockSpec(memory_space=pltpu.HBM)],
        out_specs=[VMEM] * len(pieces),
        out_shape=[pltpu.VMEM((per, size, width // parts), grads.dtype) for _, _, size in pieces],
        scratch_shapes=[pltpu.SemaphoreType.DMA((len(pieces),))],
        compiler_params=pltpu.CompilerParams(vmem_limit_bytes=4 << 20),
        name="cut",
    )(pltpu.with_memory_space_constraint(grads, pltpu.HBM))
    return [near(c) for c in cuts]


def near(value):
    return pltpu.with_memory_space_constraint(value, pltpu.VMEM)


def shift(value, axis, by):
    n = lax.axis_size(axis)
    return near(lax.ppermute(value, axis, [(i, (i + by) % n) for i in range(n)]))


def shards(grads, order):
    per, rows, width = grads.shape
    parts, devices = lax.axis_size("task"), lax.axis_size(TASK_PARAM)
    entries = rows * lax.axis_size(PARAM) * width
    sent = {}
    for pieces in GROUPS:
        for piece, c in zip(pieces, cut(grads, parts, pieces)):
            sent[piece] = shift(c, "task", piece[0])
    own = cut(grads, parts, ((0, 0, rows),))[0]
    chunks, row0 = [], 0
    for size in CHUNKS:
        chunk = [(own, row0)]
        for s in SHIFTS:
            for (by, top, height), block in sent.items():
                if by == s and top <= row0 < top + height:
                    chunk.append((block, row0 - top))
        chunks.append(chunk)
        row0 += size
    gram, tables_of = None, None
    for k, (chunk, size) in enumerate(zip(chunks, CHUNKS)):
        gram, *more = gram_of(order, chunk, size, gram, devices, k == len(CHUNKS) - 1)
        tables_of = more or tables_of
    gram = lax.all_to_all(gram, TASK_PARAM, 0, 0, tiled=True)
    update, poor, scale = combine(gram, tables_of, chunks, CHUNKS, entries)

    def normalize(update):
        energy = functools.reduce(lax.psum, TASK_PARAM, jnp.sum(update * update))
        return update * (0.5 / jnp.sqrt(energy / entries + EPS * scale[0] * scale[0]))

    return lax.cond(poor[0] > 0.0, normalize, lambda update: update, update)


def solution(mesh):
    torus = Mesh(
        mesh.devices.reshape(mesh.shape["task"], 4, 4, 2), ("task", "param_0", "param_1", "param_2")
    )
    in_specs = (P("task", PARAM, None), P())
    out_specs = P(PARAM, "task")
    return jax.shard_map(
        shards, mesh=torus, in_specs=in_specs, out_specs=out_specs, check_vma=False
    )
```

```python
import functools

import jax
import jax.numpy as jnp
from jax import lax
from jax.experimental import pallas as pl
from jax.experimental.pallas import tpu as pltpu
from jax.sharding import Mesh
from jax.sharding import PartitionSpec as P

PARAM = ("param_0", "param_1", "param_2")
TASK_PARAM = ("task", *PARAM)
CHUNKS = (208, 48)
SHIFTS = (2, 1, 3)
GROUPS = (((2, 0, 256),), ((1, 0, 208), (3, 0, 208)), ((1, 208, 48), (3, 208, 48)))
GRAIN = 16
OUT_ROWS = 64
LANES = 128
SUBLANES = 8
EPS = 1e-06
CANCEL = 0.001
VMEM = pl.BlockSpec(memory_space=pltpu.VMEM)
SMEM = pl.BlockSpec(memory_space=pltpu.SMEM)


def slot_tasks(parts, per):
    me = lax.axis_index("task")
    return [lax.rem(me + (parts - s), parts) * per + u for s in (0, *SHIFTS) for u in range(per)]


def tables(order_ref, slots, rows_ref, columns_ref, pick_ref):
    tasks = len(slots)

    def ordered(shape, dim):
        place, task = lax.broadcasted_iota(jnp.int32, shape, dim), jnp.full(shape, -1, jnp.int32)
        for k in range(tasks):
            task = jnp.where(place == k, order_ref[k], task)
        return task

    lane = lax.broadcasted_iota(jnp.int32, rows_ref.shape, 1)
    rows_ref[...] = jnp.where(lane // tasks == ordered(rows_ref.shape, 0), 1.0, 0.0)
    sub = lax.broadcasted_iota(jnp.int32, columns_ref.shape, 0)
    columns_ref[...] = jnp.where(sub % tasks == ordered(columns_ref.shape, 1), 1.0, 0.0)
    for i, task in enumerate(slots):
        pick_ref[i] = jnp.where(ordered(pick_ref.shape[1:], 0) == task, 1.0, 0.0)


def pieces_of(value):
    high = value.astype(jnp.bfloat16)
    rest = value - high.astype(jnp.float32)
    middle = rest.astype(jnp.bfloat16)
    return high, middle, (rest - middle.astype(jnp.float32)).astype(jnp.bfloat16)


def exact_dot(x, y, contract):
    return lax.dot_general(x, y, (contract, ((), ())), preferred_element_type=jnp.float32)


def gram_kernel(parts, per, rows, bases, first, last, *refs):
    if first:
        order_ref, refs = refs[0], refs[1:]
    blocks, refs = refs[:parts], refs[parts:]
    if not first:
        before_ref, refs = refs[0], refs[1:]
    out_ref, *refs = refs
    acc_ref = refs[-1] if last else out_ref
    tasks = parts * per
    width = blocks[0].shape[2]
    slots = slot_tasks(parts, per)
    pairs = [(i, j) for i in range(tasks) for j in range(i, tasks)]

    def body(r, sums):
        sums = list(sums)
        for c in range(width // LANES):
            cols = pl.ds(c * LANES, LANES)
            x = [
                b[u, pl.ds(base + r * GRAIN, GRAIN), cols].astype(jnp.float32)
                for b, base in zip(blocks, bases)
                for u in range(per)
            ]
            for h in range(GRAIN // SUBLANES):
                part = [v[h * SUBLANES : (h + 1) * SUBLANES] for v in x]
                for p, (i, j) in enumerate(pairs):
                    sums[p] = sums[p] + part[i] * part[j]
        return tuple(sums)

    zero = jnp.zeros((SUBLANES, LANES), jnp.float32)
    sums = lax.fori_loop(0, rows // GRAIN, body, (zero,) * len(pairs))
    square = tasks * tasks
    for p, (i, j) in enumerate(pairs):
        for a, b in ((i, j), (j, i))[: 1 if i == j else 2]:
            acc_ref[pl.ds(slots[a] * tasks + slots[b], SUBLANES, stride=square), :] = sums[p]
    if not first:
        acc_ref[...] += before_ref[...]
    if first:
        tables(order_ref, slots, *refs[:3])
    if last:
        folded = acc_ref[:square, :]
        for k in range(1, SUBLANES):
            folded = folded + acc_ref[k * square : (k + 1) * square, :]
        high, middle, low = pieces_of(folded)
        ones = jnp.ones((GRAIN, LANES), jnp.bfloat16)
        row = exact_dot(ones, jnp.concatenate([high, middle], axis=0), ((1,), (1,)))
        row += exact_dot(ones, jnp.concatenate([jnp.zeros_like(low), low], axis=0), ((1,), (1,)))
        out_ref[...] = jnp.broadcast_to(row[:1], out_ref.shape)


def gram_of(order, chunk, rows, before, devices, last):
    blocks, bases = zip(*chunk)
    parts, per = len(blocks), blocks[0].shape[0]
    tasks = parts * per
    table = (SUBLANES * tasks**2, LANES)
    first = before is None
    shapes = [(devices, LANES) if last else table]
    if first:
        shapes += [(tasks, LANES), (LANES, LANES), (tasks, tasks, LANES)]
    return pl.pallas_call(
        functools.partial(gram_kernel, parts, per, rows, bases, first, last),
        in_specs=[SMEM] * first + [VMEM] * (parts + (not first)),
        out_specs=[VMEM] * len(shapes),
        out_shape=[jax.ShapeDtypeStruct(shape, jnp.float32) for shape in shapes],
        scratch_shapes=[pltpu.VMEM(table, jnp.float32)] if last else [],
        compiler_params=pltpu.CompilerParams(vmem_limit_bytes=4 << 20),
        name="gram",
    )(*([order] if first else []), *blocks, *([] if first else [before]))


def combine_kernel(per, entries, chunks, gram_ref, rows_ref, columns_ref, pick_ref, *refs):
    refs, (out_ref, poor_ref, scale_ref, total_ref, sems) = refs[:-5], refs[-5:]
    tasks = rows_ref.shape[0]
    flat = jnp.sum(gram_ref[...], axis=0, keepdims=True)
    flat = flat + pltpu.roll(flat, tasks * tasks, 1)
    pieces = [p.astype(jnp.float32) for p in pieces_of(flat)]
    spread = jnp.concatenate([rows_ref[...] * p for p in pieces], axis=0).astype(jnp.bfloat16)
    found = exact_dot(spread, columns_ref[...].astype(jnp.bfloat16), ((1,), (0,)))
    gram = found[2 * tasks :] + found[tasks : 2 * tasks] + found[:tasks]
    lane = lax.broadcasted_iota(jnp.int32, (tasks, LANES), 1)
    sub = lax.broadcasted_iota(jnp.int32, (tasks, LANES), 0)
    eye = lane == sub
    norm = jnp.sum(jnp.where(eye, gram, 0.0), axis=1, keepdims=True)
    inverse = jnp.broadcast_to(1.0 / (norm + EPS), (tasks, LANES))
    columns = [jnp.broadcast_to(gram[:, k : k + 1], (tasks, LANES)) for k in range(tasks)]
    coefs, dots = eye.astype(jnp.float32), gram
    for k in range(tasks):
        w = jnp.minimum(dots[k : k + 1, :], 0.0) * inverse[k : k + 1, :]
        w = jnp.broadcast_to(jnp.where(lane[:1] == k, 0.0, w), (tasks, LANES))
        coefs = coefs - jnp.where(sub == k, w, 0.0)
        dots = dots - columns[k] * w
    weight = jnp.sum(coefs, axis=1, keepdims=True)
    energy = jnp.sum(weight * jnp.sum(dots, axis=1, keepdims=True), axis=0, keepdims=True)
    least = jnp.sum(jnp.abs(weight) * jnp.sqrt(jnp.maximum(norm, 0.0)), axis=0, keepdims=True)
    least = least * least * CANCEL
    scale = 0.5 / jnp.sqrt(jnp.maximum(energy, least) / entries + EPS)
    poor_ref[...] = jnp.broadcast_to(least - energy, (1, LANES)).reshape(LANES)
    scale_ref[...] = jnp.broadcast_to(scale, (1, LANES)).reshape(LANES)
    weight = jnp.broadcast_to(weight * scale, (tasks, LANES))
    weights = [
        jnp.broadcast_to(jnp.sum(pick_ref[i] * weight, axis=0, keepdims=True), (GRAIN, LANES))
        for i in range(tasks)
    ]
    width = total_ref.shape[1]
    copies = []
    for row0, size, places_of in chunks:
        blocks = [(refs[k], base) for k, base in places_of]
        for top in range(0, size, OUT_ROWS):
            here = min(OUT_ROWS, size - top)

            def body(r, _):
                at = pl.multiple_of(top + r * GRAIN, GRAIN)
                for c in range(0, width, LANES):
                    cols = pl.ds(c, LANES)
                    total = None
                    for i, weight in enumerate(weights):
                        block, base = blocks[i // per]
                        x = block[i % per, pl.ds(base + at, GRAIN), cols]
                        term = weight * x.astype(jnp.float32)
                        total = term if total is None else total + term
                    total_ref[pl.ds(row0 + at, GRAIN), cols] = total
                return 0

            lax.fori_loop(0, here // GRAIN, body, 0)
            span = pl.ds(row0 + top, here)
            copy = pltpu.make_async_copy(total_ref.at[span], out_ref.at[span], sems.at[len(copies)])
            copy.start()
            copies.append(copy)
    for copy in copies:
        copy.wait()


def combine(gram, tables_of, chunks, sizes, entries):
    blocks, layout, row0 = [], [], 0
    for chunk, size in zip(chunks, sizes):
        found = []
        for block, base in chunk:
            known = [k for k, b in enumerate(blocks) if b is block]
            if not known:
                blocks.append(block)
            found.append((known[0] if known else len(blocks) - 1, base))
        layout.append((row0, size, tuple(found)))
        row0 += size
    per, _, width = blocks[0].shape
    return pl.pallas_call(
        functools.partial(combine_kernel, per, entries, tuple(layout)),
        in_specs=[VMEM] * (1 + len(tables_of) + len(blocks)),
        out_specs=[pl.BlockSpec(memory_space=pltpu.HBM), VMEM, VMEM],
        out_shape=[
            pltpu.HBM((row0, width), jnp.float32),
            jax.ShapeDtypeStruct((LANES,), jnp.float32),
            jax.ShapeDtypeStruct((LANES,), jnp.float32),
        ],
        scratch_shapes=[
            pltpu.VMEM((row0, width), jnp.float32),
            pltpu.SemaphoreType.DMA((sum(-(-size // OUT_ROWS) for size in sizes),)),
        ],
        compiler_params=pltpu.CompilerParams(vmem_limit_bytes=4 << 20),
        name="combine",
    )(gram, *tables_of, *blocks)


def cut_kernel(parts, pieces, grads_ref, *refs):
    outs, sems = refs[:-1], refs[-1]
    me = lax.axis_index("task")
    copies = []
    for k, (s, row0, size) in enumerate(pieces):
        block = outs[k].shape[-1]
        column = pl.multiple_of(lax.rem(me + s, parts) * block, block)
        source = grads_ref.at[:, pl.ds(row0, size), pl.ds(column, block)]
        copies.append(pltpu.make_async_copy(source, outs[k], sems.at[k]))
    for copy in copies:
        copy.start()
    for copy in copies:
        copy.wait()


def cut(grads, parts, pieces):
    per, _, width = grads.shape
    cuts = pl.pallas_call(
        functools.partial(cut_kernel, parts, pieces),
        in_specs=[pl.BlockSpec(memory_space=pltpu.HBM)],
        out_specs=[VMEM] * len(pieces),
        out_shape=[pltpu.VMEM((per, size, width // parts), grads.dtype) for _, _, size in pieces],
        scratch_shapes=[pltpu.SemaphoreType.DMA((len(pieces),))],
        compiler_params=pltpu.CompilerParams(vmem_limit_bytes=4 << 20),
        name="cut",
    )(pltpu.with_memory_space_constraint(grads, pltpu.HBM))
    return [near(c) for c in cuts]


def near(value):
    return pltpu.with_memory_space_constraint(value, pltpu.VMEM)


def shift(value, axis, by):
    n = lax.axis_size(axis)
    return near(lax.ppermute(value, axis, [(i, (i + by) % n) for i in range(n)]))


def shards(grads, order):
    per, rows, width = grads.shape
    parts, devices = lax.axis_size("task"), lax.axis_size(TASK_PARAM)
    entries = rows * lax.axis_size(PARAM) * width
    sent = {}
    for pieces in GROUPS:
        for piece, c in zip(pieces, cut(grads, parts, pieces)):
            sent[piece] = shift(c, "task", piece[0])
    own = cut(grads, parts, ((0, 0, rows),))[0]
    chunks, row0 = [], 0
    for size in CHUNKS:
        chunk = [(own, row0)]
        for s in SHIFTS:
            for (by, top, height), block in sent.items():
                if by == s and top <= row0 < top + height:
                    chunk.append((block, row0 - top))
        chunks.append(chunk)
        row0 += size
    gram, tables_of = None, None
    for k, (chunk, size) in enumerate(zip(chunks, CHUNKS)):
        gram, *more = gram_of(order, chunk, size, gram, devices, k == len(CHUNKS) - 1)
        tables_of = more or tables_of
    gram = lax.all_to_all(gram, TASK_PARAM, 0, 0, tiled=True)
    update, poor, scale = combine(gram, tables_of, chunks, CHUNKS, entries)

    def normalize(update):
        energy = functools.reduce(lax.psum, TASK_PARAM, jnp.sum(update * update))
        return update * (0.5 / jnp.sqrt(energy / entries + EPS * scale[0] * scale[0]))

    return lax.cond(poor[0] > 0.0, normalize, lambda update: update, update)


def solution(mesh):
    torus = Mesh(
        mesh.devices.reshape(mesh.shape["task"], 4, 4, 2), ("task", "param_0", "param_1", "param_2")
    )
    in_specs = (P("task", PARAM, None), P())
    out_specs = P(PARAM, "task")
    return jax.shard_map(
        shards, mesh=torus, in_specs=in_specs, out_specs=out_specs, check_vma=False
    )
```
